256 devices in a mesh: gx: 32 (over y, z), gy: 8 (over x, core).
Axes of the slice: x: 4, y: 4, z: 8, core: 2. Of those that a mesh axis runs over, the one named last changes fastest.
Arguments:
- density_init: float32 [2, 1024, 512, 128], P(None, 'gx', 'gy'), may hold values from 0.2 to 1.5
- solid_mask: int32 [1024, 512, 128], P('gx', 'gy'), may hold values from 0 to 1
- loadings: float32 [2], replicated, may hold values from 0.3 to 1
Outputs:
- density: float32 [2, 1024, 512, 128], P(None, 'gx', 'gy')
The draws below stay inside these ranges and needn't reach their ends.
All inputs are finite; a program needn't handle non-finite values.
Results may differ from the reference program's by a relative error of at most 0.0001.
Values sent between devices are 32-bit elements; how exact they have to be, the bound alone decides.
A program may use at most 128 MiB of HBM per device.

```python
import math
import jax
import jax.numpy as jnp
import numpy as np
from jax import lax

NZ = 128
ITERS = 2
NX = 1024
NY = 512


def draw_solid_mask(key, part):
    rows = jnp.arange(NX, dtype=jnp.int32)[:, None, None]
    levels = jax.random.randint(key, (NX, NY, NZ), 0, 4, dtype=jnp.int32)
    limits = 1 + 3 * rows // NX
    return (levels >= limits).astype(jnp.int32)


def block_levels(rng, extent, shards, smallest, high):
    def one(position, shards_of):
        steps = jax.random.uniform(jax.random.fold_in(jax.random.fold_in(rng, 6), position), (shards_of,), jnp.float32, smallest / len(shards), high / len(shards))
        return jnp.repeat(jnp.exp(steps), extent[position] // shards_of).reshape((-1,) + (1,) * (len(extent) - position - 1))

    factor_of = one(*shards[0])
    for cut in shards[1:]:
        factor_of = factor_of * one(*cut)
    return factor_of


def setup_inputs(seed: int = 0) -> dict:
    keys = jax.random.split(jax.random.key(seed), 4)
    density_init = jnp.clip(0.2 + 1.3 * jax.random.uniform(keys[0], (2, NX, NY, NZ), jnp.float32) ** block_levels(keys[0], (2, NX, NY, NZ), ((1, 32), (2, 8)), -0.2, 0.2), 0.2, 1.5)
    solid_mask = draw_solid_mask(jax.random.fold_in(keys[3], 71), 0)
    loadings = jnp.clip(jnp.exp(jax.random.uniform(keys[2], (2,), jnp.float32, math.log(0.3), math.log(1.0))), 0.3, 1.0)
    return {"density_init": density_init, "solid_mask": solid_mask, "loadings": loadings}


SEGMENTS = (1.5131, 1.0)
RADII = (6.0, 8.0)
CROSS = 0.25
DAMPING = 0.3
ATTRACT = ((0.30, 0.22), (0.22, 0.16))


def profile(kind, radius):
    offset = np.arange(17) - 8.0
    if kind == 0:
        values = np.maximum(radius * radius - offset * offset, 0.0)
    elif kind == 1:
        values = offset * offset * np.maximum(radius * radius - offset * offset, 0.0)
    else:
        values = np.exp(-np.abs(offset) / 4.0)
    return values / values.sum()


def smooth_axis(field, taps_row, axis):
    widths = [(0, 0), (0, 0), (0, 0)]
    widths[axis] = (8, 8)
    padded = jnp.pad(field, widths)
    length = field.shape[axis]
    total = jnp.zeros_like(field)
    for offset in range(17):
        total = total + float(taps_row[offset]) * lax.slice_in_dim(padded, offset, offset + length, axis=axis)
    return total


def convolve(field, taps_row):
    return smooth_axis(smooth_axis(smooth_axis(field, taps_row, 0), taps_row, 1), taps_row, 2)


def reference(density_init, solid_mask, loadings):
    pore_mask = (solid_mask == 0).astype(jnp.float32)
    density = density_init * pore_mask[None]
    total_cells = float(NX * NY * NZ)
    for iteration in range(ITERS):
        packing = SEGMENTS[0] * convolve(density[0], profile(0, RADII[0])) + SEGMENTS[1] * convolve(density[1], profile(0, RADII[1]))
        surface = convolve(density[0], profile(1, RADII[0])) + convolve(density[1], profile(1, RADII[1]))
        attraction = [convolve(density[0], profile(2, 0.0)), convolve(density[1], profile(2, 0.0))]
        deriv_two = jnp.log(1.0 + packing) + 2.0 * CROSS * surface * (1.0 + packing)
        deriv_three = surface / (1.0 + packing) + CROSS * surface * surface
        proposals = []
        for comp in range(2):
            potential = SEGMENTS[comp] * convolve(deriv_three, profile(0, RADII[comp])) + convolve(deriv_two, profile(1, RADII[comp]))
            potential = potential - ATTRACT[comp][0] * attraction[0] - ATTRACT[comp][1] * attraction[1]
            proposals.append(pore_mask * jnp.exp(-potential))
        proposal = jnp.stack(proposals)
        totals = jnp.sum(proposal, axis=(1, 2, 3))
        scales = loadings * total_cells / totals
        density = (1.0 - DAMPING) * density + DAMPING * scales[:, None, None, None] * proposal
    return density
```

```python
import functools

import jax
import jax.numpy as jnp
import ml_dtypes
import numpy as np
from jax import lax
from jax.experimental import pallas as pl
from jax.experimental.pallas import tpu as pltpu
from jax.sharding import PartitionSpec as P

ITERS = 2
SEGMENTS = (1.5131, 1.0)
RADII = (6.0, 8.0)
CROSS = 0.25
DAMPING = 0.3
ATTRACT = ((0.3, 0.22), (0.22, 0.16))

W = 8
ROWS, COLS, DEPTH = 32, 64, 128
PR, PC = ROWS + 2 * W, COLS + 2 * W
BLK = 8
GX, GY, NZ_, NY_ = 32, 8, 8, 4
MESH = pl.DeviceIdType.MESH
BF16 = jnp.bfloat16
F32 = jnp.float32


def raw_profile(kind, radius):
    k = np.arange(17) - 8.0
    if kind == 0:
        return np.maximum(radius * radius - k * k, 0.0)
    if kind == 1:
        return k * k * np.maximum(radius * radius - k * k, 0.0)
    v = np.exp(-np.abs(k) / 4.0)
    return v / v.sum()


RAW = {(k, c): raw_profile(k, RADII[c]) for k in range(3) for c in range(2)}


def x_taps(kind, comp, extra=1.0):
    v = RAW[kind, comp]
    return (v / v.sum() ** 3 * extra).tolist()


def split_np(table):
    hi = table.astype(np.float32).astype(ml_dtypes.bfloat16)
    lo = (table - hi.astype(np.float64)).astype(np.float32).astype(ml_dtypes.bfloat16)
    return hi, lo


def band_y(profiles):
    tables = []
    for taps in profiles:
        t = np.zeros((COLS, PC))
        for o in range(COLS):
            t[o, o : o + 17] = taps
        tables.append(t)
    hi, lo = split_np(np.concatenate(tables, 0))
    pad = np.zeros((hi.shape[0], 16), ml_dtypes.bfloat16)
    return np.concatenate([hi, hi, lo, pad], 1)


def band_z(taps):
    t = np.zeros((DEPTH, DEPTH))
    for o in range(DEPTH):
        for k in range(17):
            i = o + k - 8
            if 0 <= i < DEPTH:
                t[i, o] = taps[k]
    return t


def stack_z(table):
    hi, lo = split_np(table)
    return np.concatenate([hi, hi, lo], 0)


def constants():
    ya = [band_y([RAW[0, c], RAW[1, c], RAW[2, c]]) for c in range(2)]
    yb = [band_y([RAW[k, 0], RAW[k, 1]]) for k in (1, 0)]
    zp = stack_z(np.concatenate([band_z(RAW[0, 0]), band_z(RAW[0, 1])], 0))[: 4 * DEPTH]
    zs = stack_z(np.concatenate([band_z(RAW[1, 0]), band_z(RAW[1, 1])], 0))
    a = band_z(RAW[2, 0])
    za = stack_z(
        np.concatenate(
            [np.concatenate([ATTRACT[i][j] * a for i in range(2)], 1) for j in range(2)], 0
        )
    )
    zm = [
        stack_z(np.concatenate([band_z(RAW[0, i]), band_z(RAW[1, i])], 0)) for i in range(2)
    ]
    return [np.stack(ya), np.stack(yb), zp, zs, za, np.stack(zm)]


def split(v):
    hi = v.astype(BF16)
    return hi, (v - hi.astype(F32)).astype(BF16)


def kernel(
    dens_hbm, mask_hbm, load_ref, ya_ref, yb_ref, zp_ref, zs_ref, za_ref, zm_ref,
    out_ref,
    rho, prp, der1, der2, mask, yf, lh, res, att, tot, scl, arbuf, arrecv,
    in_sem, hs, hr, cs, cr, as_, ar_,
):
    gx, gy = lax.axis_index("gx"), lax.axis_index("gy")
    yy, zz = gx // NZ_, gx % NZ_
    cells = float(ROWS * GX * COLS * GY * DEPTH)

    loads = [
        pltpu.make_async_copy(
            dens_hbm, rho.at[:, pl.ds(W, ROWS), pl.ds(W, COLS), :], in_sem.at[0]
        ),
        pltpu.make_async_copy(mask_hbm, mask, in_sem.at[1]),
    ]
    for c in loads:
        c.start()

    group_peers = (
        [(gx, (gy + d) % GY) for d in range(1, GY)]
        + [(yy * NZ_ + (zz + d) % NZ_, gy) for d in range(1, NZ_)]
        + [(((yy + d) % NY_) * NZ_ + zz, gy) for d in range(1, NY_)]
    )
    barrier = pltpu.get_barrier_semaphore()
    for peer in group_peers:
        pl.semaphore_signal(barrier, inc=1, device_id=peer, device_id_type=MESH)

    has_lo, has_hi = gx > 0, gx < GX - 1
    has_l, has_r = gy > 0, gy < GY - 1

    @pl.when(has_lo)
    def _():
        pl.semaphore_signal(barrier, inc=1, device_id=(gx - 1, gy), device_id_type=MESH)

    @pl.when(has_hi)
    def _():
        pl.semaphore_signal(barrier, inc=1, device_id=(gx + 1, gy), device_id_type=MESH)

    for buf in (rho, prp, der1, der2):
        @pl.when(gx == 0)
        def _(buf=buf):
            buf[:, pl.ds(0, W)] = jnp.zeros((2, W, PC, DEPTH), F32)

        @pl.when(gx == GX - 1)
        def _(buf=buf):
            buf[:, pl.ds(W + ROWS, W)] = jnp.zeros((2, W, PC, DEPTH), F32)

        @pl.when(gy == 0)
        def _(buf=buf):
            buf[:, :, pl.ds(0, W)] = jnp.zeros((2, PR, W, DEPTH), F32)

        @pl.when(gy == GY - 1)
        def _(buf=buf):
            buf[:, :, pl.ds(W + COLS, W)] = jnp.zeros((2, PR, W, DEPTH), F32)

    for c in loads:
        c.wait()

    def mask_row(x, carry):
        keep = mask[x] == 0
        for c in range(2):
            v = rho[c, x + W, pl.ds(W, COLS), :]
            rho[c, x + W, pl.ds(W, COLS), :] = jnp.where(keep, v, 0.0)
        return carry

    lax.fori_loop(0, ROWS, mask_row, 0)

    pl.semaphore_wait(
        barrier, len(group_peers) + has_lo.astype(jnp.int32) + has_hi.astype(jnp.int32)
    )

    def copy(buf, src, dst, send, recv, peer):
        return pltpu.make_async_remote_copy(
            src_ref=buf.at[(slice(None),) + src],
            dst_ref=buf.at[(slice(None),) + dst],
            send_sem=send,
            recv_sem=recv,
            device_id=peer,
            device_id_type=MESH,
        )

    def exchange(n, buf, w):
        own_x, own_y = pl.ds(W, ROWS), pl.ds(W, COLS)
        lo_src, hi_src = pl.ds(W, w), pl.ds(W + ROWS - w, w)
        lo_dst, hi_dst = pl.ds(W - w, w), pl.ds(W + ROWS, w)
        l_src, r_src = pl.ds(W, W), pl.ds(COLS, W)
        l_dst, r_dst = pl.ds(0, W), pl.ds(W + COLS, W)
        down, up = (gx - 1, gy), (gx + 1, gy)
        left, right = (gx, gy - 1), (gx, gy + 1)
        faces = [
            (copy(buf, (lo_src, own_y), (hi_dst, own_y), hs.at[n, 0], hr.at[n, 0], down), has_lo, has_hi),
            (copy(buf, (hi_src, own_y), (lo_dst, own_y), hs.at[n, 1], hr.at[n, 1], up), has_hi, has_lo),
            (copy(buf, (own_x, l_src), (own_x, r_dst), hs.at[n, 2], hr.at[n, 2], left), has_l, has_r),
            (copy(buf, (own_x, r_src), (own_x, l_dst), hs.at[n, 3], hr.at[n, 3], right), has_r, has_l),
        ]
        corners = []
        for i, (rows, has_x) in enumerate(((lo_dst, has_lo), (hi_dst, has_hi))):
            corners.append(
                (copy(buf, (rows, l_src), (rows, r_dst), cs.at[n, 2 * i], cr.at[n, 2 * i], left),
                 has_x & has_l, has_x & has_r)
            )
            corners.append(
                (copy(buf, (rows, r_src), (rows, l_dst), cs.at[n, 2 * i + 1], cr.at[n, 2 * i + 1], right),
                 has_x & has_r, has_x & has_l)
            )
        return faces, corners

    def start(items):
        for c, to, _ in items:
            pl.when(to)(c.start)

    def wait_recv(items):
        for c, _, frm in items:
            pl.when(frm)(c.wait_recv)

    def wait_send(items):
        for c, to, _ in items:
            pl.when(to)(c.wait_send)

    def conv_y(buf, band_ref, order, lo, hi):
        def pair(p, carry):
            x = 2 * p
            for ch, fields in order:
                columns = []
                for j in range(2):
                    h, l = split(buf[ch, x + j])
                    columns.append(jnp.concatenate([h, l, h, h[:16]], 0))
                rhs = jnp.concatenate(columns, 1)
                out = jnp.dot(band_ref[ch], rhs, preferred_element_type=F32)
                for q, f in enumerate(fields):
                    for j in range(2):
                        yf[f, x + j] = out[q * COLS : (q + 1) * COLS, j * DEPTH : (j + 1) * DEPTH]
            return carry

        lax.fori_loop(lo, hi, pair, 0)

    def conv_x(b, specs):
        def chunk(j, carry):
            cols = pl.ds(pl.multiple_of(j * 16, 16), 16)
            for f, taps, radius, kind, column in specs:
                rows = {
                    i: yf[f, b * BLK + W + i, cols, :] for i in range(-radius, BLK + radius)
                }
                for x in range(BLK):
                    acc = None
                    for k in range(radius + 1):
                        w = taps[8 + k]
                        if w == 0.0:
                            continue
                        v = rows[x] if k == 0 else rows[x + k] + rows[x - k]
                        acc = w * v if acc is None else acc + w * v
                    h, l = split(acc)
                    at = pl.ds(pl.multiple_of(x * COLS + j * 16, 16), 16)
                    lh[kind, 0, at, pl.ds(column * DEPTH, DEPTH)] = h
                    lh[kind, 1, at, pl.ds(column * DEPTH, DEPTH)] = l
            return carry

        lax.fori_loop(0, COLS // 16, chunk, 0)

    def conv_z(kind, band_ref_value, terms):
        h, l = lh[kind, 0], lh[kind, 1]
        lhs = jnp.concatenate([h, l, h][:terms], 1)
        return jnp.dot(lhs, band_ref_value, preferred_element_type=F32)

    specs_a = []
    for c, r in ((0, 5), (1, 7)):
        specs_a.append((c * 3 + 0, x_taps(0, c, SEGMENTS[c]), r, 0, c))
        specs_a.append((c * 3 + 1, x_taps(1, c), r, 1, c))
        specs_a.append((c * 3 + 2, x_taps(2, c), 8, 2, c))
    specs_b = []
    for c, r in ((0, 5), (1, 7)):
        specs_b.append((2 + c, x_taps(0, c, SEGMENTS[c]), r, c, 0))
        specs_b.append((c, x_taps(1, c), r, c, 1))

    def stage_a(b, der):
        conv_x(b, specs_a)
        res[0] = conv_z(0, zp_ref[...], 2)
        res[1] = conv_z(1, zs_ref[...], 3)
        both = conv_z(2, za_ref[...], 3)
        at = pl.ds(pl.multiple_of(b * BLK * COLS, BLK * COLS), BLK * COLS)
        att[0, at] = both[:, :DEPTH]
        att[1, at] = both[:, DEPTH:]

        def row(x, carry):
            at = pl.ds(pl.multiple_of(x * COLS, COLS), COLS)
            t = 1.0 + res[0, at]
            n2 = res[1, at]
            der[0, b * BLK + x + W, pl.ds(W, COLS), :] = jnp.log(t) + (2.0 * CROSS) * n2 * t
            der[1, b * BLK + x + W, pl.ds(W, COLS), :] = n2 / t + CROSS * n2 * n2
            return carry

        lax.fori_loop(0, BLK, row, 0)

    def stage_b(b):
        conv_x(b, specs_b)
        for i in range(2):
            res[i] = conv_z(i, zm_ref[i], 3)

        def row(x, carry):
            at = pl.ds(pl.multiple_of(x * COLS, COLS), COLS)
            glob = pl.ds(pl.multiple_of((b * BLK + x) * COLS, COLS), COLS)
            keep = mask[b * BLK + x] == 0
            for i in range(2):
                v = jnp.where(keep, jnp.exp(att[i, glob] - res[i, at]), 0.0)
                prp[i, b * BLK + x + W, pl.ds(W, COLS), :] = v
                part = v[0:8]
                for q in range(1, COLS // 8):
                    part = part + v[8 * q : 8 * q + 8]
                tot[i] = tot[i] + part
            return carry

        lax.fori_loop(0, BLK, row, 0)

    def total_scales(it):
        sums = [jnp.sum(tot[i], axis=0, keepdims=True) for i in range(2)]
        rowid = lax.broadcasted_iota(jnp.int32, (8, DEPTH), 0)
        mine = jnp.where(rowid == 0, sums[0], jnp.where(rowid == 1, sums[1], 0.0))
        stages = [
            [(gx, (gy + d) % GY) for d in range(1, GY)],
            [(yy * NZ_ + (zz + d) % NZ_, gy) for d in range(1, NZ_)],
            [(((yy + d) % NY_) * NZ_ + zz, gy) for d in range(1, NY_)],
        ]
        copies = []
        for s, peers in enumerate(stages):
            arbuf[it, s] = mine
            sent = []
            for d, peer in enumerate(peers):
                c = pltpu.make_async_remote_copy(
                    src_ref=arbuf.at[it, s],
                    dst_ref=arrecv.at[it, s, d],
                    send_sem=as_.at[it, s, d],
                    recv_sem=ar_.at[it, s, d],
                    device_id=peer,
                    device_id_type=MESH,
                )
                c.start()
                sent.append(c)
            for d, c in enumerate(sent):
                c.wait_recv()
                mine = mine + arrecv[it, s, d]
            copies += sent
        total = jnp.sum(mine, axis=1, keepdims=True)
        for i in range(2):
            s = load_ref[i] * cells / total[i : i + 1]
            scl[i] = jnp.broadcast_to(s, (8, DEPTH))
        return copies

    order_a = ((0, (0, 1, 2)), (1, (3, 4, 5)))
    order_b = ((0, (0, 1)), (1, (2, 3)))
    pending = []
    ders = (der1, der2)
    source = rho
    first = exchange(0, rho, W)
    start(first[0])
    for it in range(ITERS):
        faces, corners = first
        pending += [faces, corners]
        wait_recv(faces)
        start(corners)
        if it == 1:
            wait_recv(corners)
            for c in copies:
                c.wait_send()
            wait_send(pending[0])
            wait_send(pending[1])

            def mix(x, carry):
                for c in range(2):
                    rho[c, x] = (1.0 - DAMPING) * rho[c, x] + (DAMPING * scl[c, 0:1]) * prp[c, x]
                return carry

            lax.fori_loop(0, PR, mix, 0)
        else:
            wait_recv(corners)
        conv_y(rho, ya_ref, order_a, 0, PR // 2)
        der = ders[it]
        lax.fori_loop(0, ROWS // BLK, lambda b, carry: (stage_a(b, der), carry)[1], 0)
        faces, corners = exchange(1 + 2 * it, der, W - 1)
        pending += [faces, corners]
        start(faces)
        wait_recv(faces)
        start(corners)
        wait_recv(corners)
        conv_y(der, yb_ref, order_b, 0, PR // 2)
        tot[...] = jnp.zeros_like(tot)
        if it == 1:
            wait_send(pending[4])
            wait_send(pending[5])
        lax.fori_loop(0, ROWS // BLK, lambda b, carry: (stage_b(b), carry)[1], 0)
        if it == 0:
            first = exchange(2, prp, W)
            start(first[0])
        copies = total_scales(it)
    for c in copies:
        c.wait_send()
    wait_send(pending[2])
    wait_send(pending[3])
    wait_send(pending[6])
    wait_send(pending[7])

    def final(x, carry):
        for c in range(2):
            out_ref[c, x] = (1.0 - DAMPING) * rho[c, x + W, pl.ds(W, COLS), :] + (
                DAMPING * scl[c, 0:1]
            ) * prp[c, x + W, pl.ds(W, COLS), :]
        return carry

    lax.fori_loop(0, ROWS, final, 0)


def body(density_init, solid_mask, loadings):
    consts = [jnp.asarray(c) for c in constants()]
    anyspace = pl.BlockSpec(memory_space=pl.ANY)
    vmem = pl.BlockSpec(memory_space=pltpu.VMEM)
    smem = pl.BlockSpec(memory_space=pltpu.SMEM)
    padded = pltpu.VMEM((2, PR, PC, DEPTH), F32)
    dma = pltpu.SemaphoreType.DMA
    return pl.pallas_call(
        kernel,
        out_shape=jax.ShapeDtypeStruct((2, ROWS, COLS, DEPTH), F32),
        in_specs=[anyspace, anyspace, smem] + [vmem] * len(consts),
        out_specs=vmem,
        scratch_shapes=[
            padded, padded, padded, padded,
            pltpu.VMEM((ROWS, COLS, DEPTH), jnp.int32),
            pltpu.VMEM((6, PR, COLS, DEPTH), F32),
            pltpu.VMEM((3, 2, BLK * COLS, 2 * DEPTH), BF16),
            pltpu.VMEM((2, BLK * COLS, DEPTH), F32),
            pltpu.VMEM((2, ROWS * COLS, DEPTH), F32),
            pltpu.VMEM((2, 8, DEPTH), F32),
            pltpu.VMEM((2, 8, DEPTH), F32),
            pltpu.VMEM((2, 3, 8, DEPTH), F32),
            pltpu.VMEM((2, 3, 7, 8, DEPTH), F32),
            dma((2,)),
            dma((4, 4)), dma((4, 4)), dma((4, 4)), dma((4, 4)),
            dma((2, 3, 7)), dma((2, 3, 7)),
        ],
        compiler_params=pltpu.CompilerParams(
            collective_id=0, has_side_effects=True, vmem_limit_bytes=60 * 2**20
        ),
        name="picard",
    )(density_init, solid_mask, loadings, *consts)


def solution(mesh):
    in_specs = (P(None, "gx", "gy", None), P("gx", "gy", None), P())
    out_specs = P(None, "gx", "gy", None)
    return jax.shard_map(body, mesh=mesh, in_specs=in_specs, out_specs=out_specs, check_vma=False)
```

```python
import functools

import jax
import jax.numpy as jnp
import ml_dtypes
import numpy as np
from jax import lax
from jax.experimental import pallas as pl
from jax.experimental.pallas import tpu as pltpu
from jax.sharding import PartitionSpec as P

ITERS = 2
SEGMENTS = (1.5131, 1.0)
RADII = (6.0, 8.0)
CROSS = 0.25
DAMPING = 0.3
ATTRACT = ((0.3, 0.22), (0.22, 0.16))

W = 8
ROWS, COLS, DEPTH = 32, 64, 128
PR, PC = ROWS + 2 * W, COLS + 2 * W
BLK = 8
GX, GY, NZ_, NY_ = 32, 8, 8, 4
MESH = pl.DeviceIdType.MESH
BF16 = jnp.bfloat16
F32 = jnp.float32


def raw_profile(kind, radius):
    k = np.arange(17) - 8.0
    if kind == 0:
        return np.maximum(radius * radius - k * k, 0.0)
    if kind == 1:
        return k * k * np.maximum(radius * radius - k * k, 0.0)
    v = np.exp(-np.abs(k) / 4.0)
    return v / v.sum()


RAW = {(k, c): raw_profile(k, RADII[c]) for k in range(3) for c in range(2)}


def x_taps(kind, comp, extra=1.0):
    v = RAW[kind, comp]
    return (v / v.sum() ** 3 * extra).tolist()


def split_np(table):
    hi = table.astype(np.float32).astype(ml_dtypes.bfloat16)
    lo = (table - hi.astype(np.float64)).astype(np.float32).astype(ml_dtypes.bfloat16)
    return hi, lo


def band_y(profiles):
    tables = []
    for taps in profiles:
        t = np.zeros((COLS, PC))
        for o in range(COLS):
            t[o, o : o + 17] = taps
        tables.append(t)
    hi, lo = split_np(np.concatenate(tables, 0))
    pad = np.zeros((hi.shape[0], 16), ml_dtypes.bfloat16)
    return np.concatenate([hi, hi, lo, pad], 1)


def band_z(taps):
    t = np.zeros((DEPTH, DEPTH))
    for o in range(DEPTH):
        for k in range(17):
            i = o + k - 8
            if 0 <= i < DEPTH:
                t[i, o] = taps[k]
    return t


def stack_z(table):
    hi, lo = split_np(table)
    return np.concatenate([hi, hi, lo], 0)


def constants():
    ya = [band_y([RAW[0, c], RAW[1, c], RAW[2, c]]) for c in range(2)]
    yb = [band_y([RAW[k, 0], RAW[k, 1]]) for k in (1, 0)]
    zp = stack_z(np.concatenate([band_z(RAW[0, 0]), band_z(RAW[0, 1])], 0))[: 4 * DEPTH]
    zs = stack_z(np.concatenate([band_z(RAW[1, 0]), band_z(RAW[1, 1])], 0))
    a = band_z(RAW[2, 0])
    za = stack_z(
        np.concatenate(
            [np.concatenate([ATTRACT[i][j] * a for i in range(2)], 1) for j in range(2)], 0
        )
    )
    zm = [
        stack_z(np.concatenate([band_z(RAW[0, i]), band_z(RAW[1, i])], 0)) for i in range(2)
    ]
    return [np.stack(ya), np.stack(yb), zp, zs, za, np.stack(zm)]


def split(v):
    hi = v.astype(BF16)
    return hi, (v - hi.astype(F32)).astype(BF16)


def kernel(
    dens_hbm, mask_hbm, load_ref, ya_hbm, yb_hbm, zp_hbm, zs_hbm, za_hbm, zm_hbm,
    base_ref, prop_ref, scl_ref,
    rho, prp, der1, der2, mask, yfa, yfp, yfb, lh, res, att, tot, scl, arbuf, arrecv,
    ya_ref, yb_ref, zp_ref, zs_ref, za_ref, zm_ref,
    in_sem, hs, hr, as_, ar_,
):
    gx, gy = lax.axis_index("gx"), lax.axis_index("gy")
    yy, zz = gx // NZ_, gx % NZ_
    cells = float(ROWS * GX * COLS * GY * DEPTH)

    loads = [
        pltpu.make_async_copy(
            dens_hbm, rho.at[:, pl.ds(W, ROWS), pl.ds(W, COLS), :], in_sem.at[0]
        ),
        pltpu.make_async_copy(mask_hbm, mask, in_sem.at[1]),
    ]
    tables = [
        pltpu.make_async_copy(a, b, in_sem.at[2 + i])
        for i, (a, b) in enumerate(
            (
                (ya_hbm, ya_ref), (zp_hbm, zp_ref), (zs_hbm, zs_ref),
                (za_hbm, za_ref), (yb_hbm, yb_ref), (zm_hbm, zm_ref),
            )
        )
    ]
    for c in loads + tables:
        c.start()

    stages = [
        [(gx, (gy + d) % GY) for d in range(1, GY)],
        [(yy * NZ_ + (zz + d) % NZ_, gy) for d in range(1, NZ_)],
        [(((yy + d) % NY_) * NZ_ + zz, gy) for d in range(1, NY_)],
    ]
    barrier = pltpu.get_barrier_semaphore()
    greeted = 0
    for peers in stages:
        for peer in peers:
            greeted += 1
            pl.semaphore_signal(barrier, inc=1, device_id=peer, device_id_type=MESH)

    has_lo, has_hi = gx > 0, gx < GX - 1
    has_l, has_r = gy > 0, gy < GY - 1

    @pl.when(has_lo)
    def _():
        pl.semaphore_signal(barrier, inc=1, device_id=(gx - 1, gy), device_id_type=MESH)

    @pl.when(has_hi)
    def _():
        pl.semaphore_signal(barrier, inc=1, device_id=(gx + 1, gy), device_id_type=MESH)

    for buf in (rho, prp, der1, der2):
        @pl.when(gx == 0)
        def _(buf=buf):
            buf[:, pl.ds(0, W)] = jnp.zeros((2, W, PC, DEPTH), F32)

        @pl.when(gx == GX - 1)
        def _(buf=buf):
            buf[:, pl.ds(W + ROWS, W)] = jnp.zeros((2, W, PC, DEPTH), F32)

        @pl.when(gy == 0)
        def _(buf=buf):
            buf[:, :, pl.ds(0, W)] = jnp.zeros((2, PR, W, DEPTH), F32)

        @pl.when(gy == GY - 1)
        def _(buf=buf):
            buf[:, :, pl.ds(W + COLS, W)] = jnp.zeros((2, PR, W, DEPTH), F32)

    tot[...] = jnp.zeros_like(tot)
    for c in loads:
        c.wait()

    def mask_row(x, carry):
        keep = mask[x] == 0
        for c in range(2):
            v = rho[c, x + W, pl.ds(W, COLS), :]
            rho[c, x + W, pl.ds(W, COLS), :] = jnp.where(keep, v, 0.0)
        return carry

    lax.fori_loop(0, ROWS, mask_row, 0)

    pl.semaphore_wait(
        barrier, greeted + has_lo.astype(jnp.int32) + has_hi.astype(jnp.int32)
    )

    class Exchange:
        def __init__(self, n, buf, w):
            count = [0]

            def item(src, dst, peer, to, frm):
                k = count[0]
                count[0] += 1
                c = pltpu.make_async_remote_copy(
                    src_ref=buf.at[(slice(None),) + src],
                    dst_ref=buf.at[(slice(None),) + dst],
                    send_sem=hs.at[n, k],
                    recv_sem=hr.at[n, k],
                    device_id=peer,
                    device_id_type=MESH,
                )
                return c, to, frm

            down, up = (gx - 1, gy), (gx + 1, gy)
            left, right = (gx, gy - 1), (gx, gy + 1)
            l_src, r_src = pl.ds(W, W), pl.ds(COLS, W)
            l_dst, r_dst = pl.ds(0, W), pl.ds(W + COLS, W)
            lo_dst, hi_dst = pl.ds(W - w, w), pl.ds(W + ROWS, w)
            parts = (l_src, r_src, pl.ds(2 * W, COLS - 2 * W))
            self.x = [
                [item((pl.ds(W, w), p), (hi_dst, p), down, has_lo, has_hi) for p in parts],
                [item((pl.ds(W + ROWS - w, w), p), (lo_dst, p), up, has_hi, has_lo) for p in parts],
            ]
            self.y = []
            for rows in (pl.ds(W, BLK), pl.ds(W + BLK, 2 * BLK), pl.ds(W + 3 * BLK, BLK)):
                self.y.append(
                    [
                        item((rows, l_src), (rows, r_dst), left, has_l, has_r),
                        item((rows, r_src), (rows, l_dst), right, has_r, has_l),
                    ]
                )
            self.corner = []
            for rows, has_x in ((lo_dst, has_lo), (hi_dst, has_hi)):
                self.corner.append(
                    [
                        item((rows, l_src), (rows, r_dst), left, has_x & has_l, has_x & has_r),
                        item((rows, r_src), (rows, l_dst), right, has_x & has_r, has_x & has_l),
                    ]
                )
            self.all = self.x[0] + self.x[1] + sum(self.y, []) + sum(self.corner, [])

        def send_side(self, side):
            start(self.x[side][:2])
            start(self.y[0 if side == 0 else 2])
            start(self.x[side][2:])

        def forward(self, side):
            recv(self.x[1 - side][:2])
            start(self.corner[side])

        def finish(self, side):
            recv(self.x[1 - side][2:])
            recv(self.corner[side])

    def start(items):
        for c, to, _ in items:
            pl.when(to)(c.start)

    def recv(items):
        for c, _, frm in items:
            pl.when(frm)(c.wait_recv)

    def sent(items):
        for c, to, _ in items:
            pl.when(to)(c.wait_send)

    def conv_y(buf, band_ref, yf, order, lo, hi, mixed=False):
        def pair(p, carry):
            x = 2 * p
            for ch, fields in order:
                columns = []
                for j in range(2):
                    h, l = split(buf[ch, x + j])
                    columns.append(jnp.concatenate([h, l, h, h[:16]], 0))
                rhs = jnp.concatenate(columns, 1)
                out = jnp.dot(band_ref[ch], rhs, preferred_element_type=F32)
                for q, f in enumerate(fields):
                    for j in range(2):
                        v = out[q * COLS : (q + 1) * COLS, j * DEPTH : (j + 1) * DEPTH]
                        if mixed:
                            v = (1.0 - DAMPING) * yf[f, x + j] + scl[ch, 0:1] * v
                        yf[f, x + j] = v
            return carry

        lax.fori_loop(lo, hi, pair, 0)

    def conv_x(b, yf, specs):
        def chunk(j, carry):
            cols = pl.ds(pl.multiple_of(j * 16, 16), 16)
            for f, taps, radius, kind, column in specs:
                rows = {
                    i: yf[f, b * BLK + W + i, cols, :] for i in range(-radius, BLK + radius)
                }
                for x in range(BLK):
                    acc = None
                    for k in range(radius + 1):
                        w = taps[8 + k]
                        if w == 0.0:
                            continue
                        v = rows[x] if k == 0 else rows[x + k] + rows[x - k]
                        acc = w * v if acc is None else acc + w * v
                    h, l = split(acc)
                    at = pl.ds(pl.multiple_of(x * COLS + j * 16, 16), 16)
                    lh[kind, 0, at, pl.ds(column * DEPTH, DEPTH)] = h
                    lh[kind, 1, at, pl.ds(column * DEPTH, DEPTH)] = l
            return carry

        lax.fori_loop(0, COLS // 16, chunk, 0)

    def conv_z(kind, table, terms):
        h, l = lh[kind, 0], lh[kind, 1]
        lhs = jnp.concatenate([h, l, h][:terms], 1)
        return jnp.dot(lhs, table, preferred_element_type=F32)

    specs_a = []
    for c, r in ((0, 5), (1, 7)):
        specs_a.append((c * 3 + 0, x_taps(0, c, SEGMENTS[c]), r, 0, c))
        specs_a.append((c * 3 + 1, x_taps(1, c), r, 1, c))
        specs_a.append((c * 3 + 2, x_taps(2, c), 8, 2, c))
    specs_b = []
    for c, r in ((0, 5), (1, 7)):
        specs_b.append((2 + c, x_taps(0, c, SEGMENTS[c]), r, c, 0))
        specs_b.append((c, x_taps(1, c), r, c, 1))

    def stage_a(lo, hi, der):
        def one(b, carry):
            conv_x(b, yfa, specs_a)
            res[0] = conv_z(0, zp_ref[...], 2)
            res[1] = conv_z(1, zs_ref[...], 3)
            both = conv_z(2, za_ref[...], 3)
            at = pl.ds(pl.multiple_of(b * BLK * COLS, BLK * COLS), BLK * COLS)
            att[0, at] = both[:, :DEPTH]
            att[1, at] = both[:, DEPTH:]

            def row(x, carry):
                at = pl.ds(pl.multiple_of(x * COLS, COLS), COLS)
                t = 1.0 + res[0, at]
                n2 = res[1, at]
                der[0, b * BLK + x + W, pl.ds(W, COLS), :] = jnp.log(t) + (2.0 * CROSS) * n2 * t
                der[1, b * BLK + x + W, pl.ds(W, COLS), :] = n2 / t + CROSS * n2 * n2
                return carry

            lax.fori_loop(0, BLK, row, 0)
            return carry

        lax.fori_loop(lo, hi, one, 0)

    def stage_b(lo, hi, dest, off):
        def one(b, carry):
            conv_x(b, yfb, specs_b)
            for i in range(2):
                res[i] = conv_z(i, zm_ref[i], 3)

            def row(x, carry):
                at = pl.ds(pl.multiple_of(x * COLS, COLS), COLS)
                glob = pl.ds(pl.multiple_of((b * BLK + x) * COLS, COLS), COLS)
                keep = mask[b * BLK + x] == 0
                for i in range(2):
                    v = jnp.where(keep, jnp.exp(att[i, glob] - res[i, at]), 0.0)
                    dest[i, b * BLK + x + off, pl.ds(off, COLS), :] = v
                    part = v[0:8]
                    for q in range(1, COLS // 8):
                        part = part + v[8 * q : 8 * q + 8]
                    tot[i] = tot[i] + part
                return carry

            lax.fori_loop(0, BLK, row, 0)
            return carry

        lax.fori_loop(lo, hi, one, 0)

    copies = []

    def sum_start(it, s, mine):
        arbuf[it, s] = mine
        out = []
        for d, peer in enumerate(stages[s]):
            c = pltpu.make_async_remote_copy(
                src_ref=arbuf.at[it, s],
                dst_ref=arrecv.at[it, s, d],
                send_sem=as_.at[it, s, d],
                recv_sem=ar_.at[it, s, d],
                device_id=peer,
                device_id_type=MESH,
            )
            c.start()
            out.append(c)
        copies.extend(out)
        return out

    def sum_finish(it, s, mine, out):
        for d, c in enumerate(out):
            c.wait_recv()
            mine = mine + arrecv[it, s, d]
        return mine

    def local_total():
        sums = [jnp.sum(tot[i], axis=0, keepdims=True) for i in range(2)]
        rowid = lax.broadcasted_iota(jnp.int32, (8, DEPTH), 0)
        return jnp.where(rowid == 0, sums[0], jnp.where(rowid == 1, sums[1], 0.0))

    def scales(mine, dest):
        total = jnp.sum(mine, axis=1, keepdims=True)
        for i in range(2):
            dest[i] = jnp.broadcast_to(DAMPING * load_ref[i] * cells / total[i : i + 1], (8, DEPTH))

    order_a = ((0, (0, 1, 2)), (1, (3, 4, 5)))
    order_b = ((0, (0, 1)), (1, (2, 3)))
    x_rho = Exchange(0, rho, W)
    x_der1 = Exchange(1, der1, W - 1)
    x_prp = Exchange(2, prp, W)
    x_der2 = Exchange(3, der2, W - 1)
    HALF = (0, 4), (20, 24)

    for side in range(2):
        start(x_rho.x[side][:2])
    for side in range(2):
        start(x_rho.x[side][2:])
    for part in range(3):
        start(x_rho.y[part])
    tables[0].wait()
    for part in range(3):
        recv(x_rho.y[part])
    conv_y(rho, ya_ref, yfa, order_a, 4, 12)
    x_rho.forward(0)
    x_rho.forward(1)
    conv_y(rho, ya_ref, yfa, order_a, 12, 20)
    for t in tables[1:4]:
        t.wait()
    stage_a(1, 3, der1)
    start(x_der1.y[1])
    for side in range(2):
        x_rho.finish(side)
        conv_y(rho, ya_ref, yfa, order_a, *HALF[side])
        stage_a(3 * side, 3 * side + 1, der1)
        x_der1.send_side(side)

    for t in tables[4:]:
        t.wait()
    recv(x_der1.y[1])
    conv_y(der1, yb_ref, yfb, order_b, 8, 16)
    recv(x_der1.y[0])
    conv_y(der1, yb_ref, yfb, order_b, 4, 8)
    x_der1.forward(1)
    recv(x_der1.y[2])
    conv_y(der1, yb_ref, yfb, order_b, 16, 20)
    x_der1.forward(0)
    stage_b(1, 3, prp, W)
    start(x_prp.y[1])
    for side in (1, 0):
        x_der1.finish(side)
        conv_y(der1, yb_ref, yfb, order_b, *HALF[side])
        stage_b(3 * side, 3 * side + 1, prp, W)
        x_prp.send_side(side)

    mine = local_total()
    tot[...] = jnp.zeros_like(tot)
    out = sum_start(0, 0, mine)
    recv(x_prp.y[1])
    conv_y(prp, ya_ref, yfp, order_a, 8, 16)
    mine = sum_finish(0, 0, mine, out)
    out = sum_start(0, 1, mine)
    recv(x_prp.y[2])
    recv(x_prp.y[0])
    x_prp.forward(0)
    conv_y(prp, ya_ref, yfp, order_a, 16, 20)
    mine = sum_finish(0, 1, mine, out)
    out = sum_start(0, 2, mine)
    x_prp.forward(1)
    conv_y(prp, ya_ref, yfp, order_a, 4, 8)
    mine = sum_finish(0, 2, mine, out)
    scales(mine, scl)

    def mix(x, carry):
        for f in range(6):
            yfa[f, x] = (1.0 - DAMPING) * yfa[f, x] + scl[f // 3, 0:1] * yfp[f, x]
        return carry

    lax.fori_loop(W, W + ROWS, mix, 0)
    for side in range(2):
        x_prp.finish(side)
        conv_y(prp, ya_ref, yfa, order_a, *HALF[side], mixed=True)
        stage_a(3 * side, 3 * side + 1, der2)
        x_der2.send_side(side)
    stage_a(1, 3, der2)
    start(x_der2.y[1])

    recv(x_der2.y[0])
    conv_y(der2, yb_ref, yfb, order_b, 4, 8)
    recv(x_der2.y[2])
    conv_y(der2, yb_ref, yfb, order_b, 16, 20)
    x_der2.forward(1)
    x_der2.forward(0)

    def base(x, carry):
        for c in range(2):
            new = (1.0 - DAMPING) * rho[c, x + W, pl.ds(W, COLS), :] + scl[c, 0:1] * prp[
                c, x + W, pl.ds(W, COLS), :
            ]
            base_ref[c, x] = (1.0 - DAMPING) * new
        return carry

    lax.fori_loop(0, ROWS, base, 0)
    recv(x_der2.y[1])
    conv_y(der2, yb_ref, yfb, order_b, 8, 16)
    stage_b(1, 3, prop_ref, 0)
    for side in (1, 0):
        x_der2.finish(side)
        conv_y(der2, yb_ref, yfb, order_b, *HALF[side])
        stage_b(3 * side, 3 * side + 1, prop_ref, 0)
    mine = local_total()
    for s in range(3):
        out = sum_start(1, s, mine)
        mine = sum_finish(1, s, mine, out)
    scales(mine, scl_ref)

    for x in (x_rho, x_der1, x_prp, x_der2):
        sent(x.all)
    for c in copies:
        c.wait_send()


def last_kernel(base_ref, prop_ref, scl_ref, out_hbm, buf, sem):
    step = 8
    copies = []
    for x in range(0, ROWS, step):

        def row(i, carry):
            for c in range(2):
                buf[c, i] = base_ref[c, i] + scl_ref[c, 0:1] * prop_ref[c, i]
            return carry

        lax.fori_loop(x, x + step, row, 0)
        at = pl.ds(x, step)
        c = pltpu.make_async_copy(buf.at[:, at], out_hbm.at[:, at], sem.at[x // step])
        c.start()
        copies.append(c)
    for c in copies:
        c.wait()


def body(density_init, solid_mask, loadings):
    consts = [jnp.asarray(c) for c in constants()]
    anyspace = pl.BlockSpec(memory_space=pl.ANY)
    vmem = pl.BlockSpec(memory_space=pltpu.VMEM)
    smem = pl.BlockSpec(memory_space=pltpu.SMEM)
    padded = pltpu.VMEM((2, PR, PC, DEPTH), F32)
    field = pltpu.VMEM((2, ROWS, COLS, DEPTH), F32)
    dma = pltpu.SemaphoreType.DMA
    base, prop, scl = pl.pallas_call(
        kernel,
        out_shape=(field, field, pltpu.VMEM((2, 8, DEPTH), F32)),
        in_specs=[anyspace, anyspace, smem] + [anyspace] * len(consts),
        out_specs=(vmem, vmem, vmem),
        scratch_shapes=[
            padded, padded, padded, padded,
            pltpu.VMEM((ROWS, COLS, DEPTH), jnp.int32),
            pltpu.VMEM((6, PR, COLS, DEPTH), F32),
            pltpu.VMEM((6, PR, COLS, DEPTH), F32),
            pltpu.VMEM((4, PR, COLS, DEPTH), F32),
            pltpu.VMEM((3, 2, BLK * COLS, 2 * DEPTH), BF16),
            pltpu.VMEM((2, BLK * COLS, DEPTH), F32),
            pltpu.VMEM((2, ROWS * COLS, DEPTH), F32),
            pltpu.VMEM((2, 8, DEPTH), F32),
            pltpu.VMEM((2, 8, DEPTH), F32),
            pltpu.VMEM((2, 3, 8, DEPTH), F32),
            pltpu.VMEM((2, 3, 7, 8, DEPTH), F32),
        ]
        + [pltpu.VMEM(c.shape, BF16) for c in consts]
        + [dma((8,)), dma((4, 16)), dma((4, 16)), dma((2, 3, 7)), dma((2, 3, 7))],
        compiler_params=pltpu.CompilerParams(
            collective_id=0, has_side_effects=True, vmem_limit_bytes=54 * 2**20
        ),
        name="picard",
    )(density_init, solid_mask, loadings, *consts)
    return pl.pallas_call(
        last_kernel,
        out_shape=jax.ShapeDtypeStruct((2, ROWS, COLS, DEPTH), F32),
        in_specs=[vmem, vmem, vmem],
        out_specs=anyspace,
        scratch_shapes=[field, dma((4,))],
        compiler_params=pltpu.CompilerParams(vmem_limit_bytes=4 * 2**20),
        name="last",
    )(base, prop, scl)


def solution(mesh):
    in_specs = (P(None, "gx", "gy", None), P("gx", "gy", None), P())
    out_specs = P(None, "gx", "gy", None)
    return jax.shard_map(body, mesh=mesh, in_specs=in_specs, out_specs=out_specs, check_vma=False)
```

```python
import jax
import jax.numpy as jnp
import ml_dtypes
import numpy as np
from jax import lax
from jax.experimental import pallas as pl
from jax.experimental.pallas import tpu as pltpu
from jax.sharding import PartitionSpec as P

SEGMENTS = (1.5131, 1.0)
RADII = (6.0, 8.0)
CROSS = 0.25
DAMPING = 0.3
ATTRACT = ((0.3, 0.22), (0.22, 0.16))

W = 8
ROWS, COLS, DEPTH = 32, 64, 128
PR, PC = ROWS + 2 * W, COLS + 2 * W
BLK = 8
GX, GY, NZ_, NY_ = 32, 8, 8, 4
NEAR, FAR = 0, 1
HALF = 4
DECAY = float(np.exp(-0.25))
MESH = pl.DeviceIdType.MESH
BF16 = jnp.bfloat16
F32 = jnp.float32


def raw_profile(kind, radius):
    k = np.arange(17) - 8.0
    if kind == 0:
        return np.maximum(radius * radius - k * k, 0.0)
    if kind == 1:
        return k * k * np.maximum(radius * radius - k * k, 0.0)
    v = np.exp(-np.abs(k) / 4.0)
    return v / v.sum()


RAW = {(k, c): raw_profile(k, RADII[c]) for k in range(3) for c in range(2)}


def x_taps(kind, comp, extra=1.0):
    v = RAW[kind, comp]
    return (v / v.sum() ** 3 * extra).tolist()


def split_np(table):
    hi = table.astype(np.float32).astype(ml_dtypes.bfloat16)
    lo = (table - hi.astype(np.float64)).astype(np.float32).astype(ml_dtypes.bfloat16)
    return hi, lo


def band_y(profiles):
    tables = []
    for taps in profiles:
        t = np.zeros((COLS, PC))
        for o in range(COLS):
            t[o, o : o + 17] = taps
        tables.append(t)
    hi, lo = split_np(np.concatenate(tables, 0))
    pad = np.zeros((hi.shape[0], 16), ml_dtypes.bfloat16)
    return np.concatenate([hi, hi, lo, pad], 1)


def band_z(taps):
    t = np.zeros((DEPTH, DEPTH))
    for o in range(DEPTH):
        for k in range(17):
            i = o + k - 8
            if 0 <= i < DEPTH:
                t[i, o] = taps[k]
    return t


def wide_z(table):
    hi, lo = split_np(table)
    return np.concatenate(
        [np.concatenate([hi, lo], 1), np.concatenate([hi, np.zeros_like(lo)], 1)], 0
    )


def constants():
    ya = [band_y([RAW[0, c], RAW[1, c], RAW[2, c]]) for c in range(2)]
    yb = [band_y([RAW[k, 0], RAW[k, 1]]) for k in (1, 0)]
    zp = [np.concatenate([split_np(band_z(RAW[0, c]))[0]] * 2, 0) for c in range(2)]
    zs = [wide_z(band_z(RAW[1, c])) for c in range(2)]
    za = wide_z(band_z(RAW[2, 0]) * RAW[2, 0][8])
    return [np.stack(ya), np.stack(yb), np.stack(zp), np.stack(zs), za]


def split(v):
    hi = v.astype(BF16)
    return hi, (v - hi.astype(F32)).astype(BF16)


def kernel(
    dens_hbm, mask_hbm, load_ref, ya_hbm, yb_hbm, zp_hbm, zs_hbm, za_hbm,
    base_ref, prop_ref, scl_ref,
    rho, prp, der1, der2, mask, yfa, yfb, lh, res, cres, att, tot, scl, arbuf, arrecv,
    ya_ref, yb_ref, zp_ref, zs_ref, za_ref,
    in_sem, hs, hr, as_, ar_,
):
    gx, gy = lax.axis_index("gx"), lax.axis_index("gy")
    yy, zz = gx // NZ_, gx % NZ_
    cells = float(ROWS * GX * COLS * GY * DEPTH)

    loads = [
        pltpu.make_async_copy(
            dens_hbm, rho.at[:, pl.ds(W, ROWS), pl.ds(W, COLS), :], in_sem.at[0]
        ),
        pltpu.make_async_copy(mask_hbm, mask, in_sem.at[1]),
    ]
    wanted = (
        (ya_hbm, ya_ref), (zp_hbm, zp_ref), (zs_hbm, zs_ref), (za_hbm, za_ref), (yb_hbm, yb_ref),
    )
    tables = [
        pltpu.make_async_copy(a, b, in_sem.at[2 + i]) for i, (a, b) in enumerate(wanted)
    ]
    for c in loads + tables:
        c.start()

    xx, core = gy // 2, gy % 2
    stages = [
        [(yy * NZ_ + (zz + d // 2) % NZ_, xx * 2 + (core + d) % 2) for d in range(1, 16)],
        [(((yy + d // 4) % NY_) * NZ_ + zz, ((xx + d) % 4) * 2 + core) for d in range(1, 16)],
    ]
    barrier = pltpu.get_barrier_semaphore()
    greeted = 0
    for peers in stages:
        for peer in peers:
            greeted += 1
            pl.semaphore_signal(barrier, inc=1, device_id=peer, device_id_type=MESH)

    has_lo, has_hi = gx > 0, gx < GX - 1
    has_l, has_r = gy > 0, gy < GY - 1

    near = (
        (has_lo, (gx - 1, gy)),
        (has_hi, (gx + 1, gy)),
        (has_l, (gx, gy - 1)),
        (has_r, (gx, gy + 1)),
    )
    for there, peer in near:
        @pl.when(there)
        def _(peer=peer):
            pl.semaphore_signal(barrier, inc=1, device_id=peer, device_id_type=MESH)

    def zeros(buf):
        @pl.when(gx == 0)
        def _():
            buf[:, pl.ds(0, W)] = jnp.zeros((2, W, PC, DEPTH), F32)

        @pl.when(gx == GX - 1)
        def _():
            buf[:, pl.ds(W + ROWS, W)] = jnp.zeros((2, W, PC, DEPTH), F32)

        @pl.when(gy == 0)
        def _():
            buf[:, :, pl.ds(0, W)] = jnp.zeros((2, PR, W, DEPTH), F32)

        @pl.when(gy == GY - 1)
        def _():
            buf[:, :, pl.ds(W + COLS, W)] = jnp.zeros((2, PR, W, DEPTH), F32)

    zeros(rho)
    for c in loads:
        c.wait()

    def mask_row(x, carry):
        keep = mask[x] == 0
        for c in range(2):
            v = rho[c, x + W, pl.ds(W, COLS), :]
            rho[c, x + W, pl.ds(W, COLS), :] = jnp.where(keep, v, 0.0)
        return carry

    lax.fori_loop(0, ROWS, mask_row, 0)

    pl.semaphore_wait(
        barrier, greeted + sum(there.astype(jnp.int32) for there, _ in near)
    )

    with_both = [(x & has_l, x & has_r) for x in (has_lo, has_hi)]

    class Exchange:
        def __init__(self, n, buf, w):
            count = [0]

            def item(src, dst, peer, to, frm):
                k = count[0]
                count[0] += 1
                c = pltpu.make_async_remote_copy(
                    src_ref=buf.at[(slice(None),) + src],
                    dst_ref=buf.at[(slice(None),) + dst],
                    send_sem=hs.at[n, k],
                    recv_sem=hr.at[n, k],
                    device_id=peer,
                    device_id_type=MESH,
                )
                return c, to, frm

            down, up = (gx - 1, gy), (gx + 1, gy)
            left, right = (gx, gy - 1), (gx, gy + 1)
            l_src, r_src = pl.ds(W, W), pl.ds(COLS, W)
            l_dst, r_dst = pl.ds(0, W), pl.ds(W + COLS, W)
            parts = (l_src, r_src, pl.ds(2 * W, COLS - 2 * W))
            lo_rows = ((0, HALF), (HALF, w - HALF))
            hi_rows = ((ROWS - HALF, HALF), (ROWS - w, w - HALF))
            self.x = [[], []]
            self.corner = [[], []]
            for r, k in lo_rows:
                src, dst = pl.ds(W + r, k), pl.ds(W + ROWS + r, k)
                self.x[0].append([item((src, p), (dst, p), down, has_lo, has_hi) for p in parts])
            for r, k in hi_rows:
                src, dst = pl.ds(W + r, k), pl.ds(W + r - ROWS, k)
                self.x[1].append([item((src, p), (dst, p), up, has_hi, has_lo) for p in parts])
            for side, rows, shift in ((0, hi_rows, -ROWS), (1, lo_rows, ROWS)):
                with_l, with_r = with_both[side]
                for r, k in rows:
                    at = pl.ds(W + r + shift, k)
                    self.corner[side].append(
                        [
                            item((at, l_src), (at, r_dst), left, with_l, with_r),
                            item((at, r_src), (at, l_dst), right, with_r, with_l),
                        ]
                    )
            self.y = []
            for r, k in ((0, 4), (4, 4), (8, 16), (24, 4), (28, 4)):
                at = pl.ds(W + r, k)
                self.y.append(
                    [
                        item((at, l_src), (at, r_dst), left, has_l, has_r),
                        item((at, r_src), (at, l_dst), right, has_r, has_l),
                    ]
                )
            self.all = sum(self.x[0] + self.x[1] + self.corner[0] + self.corner[1] + self.y, [])

        def send(self, side, c):
            start(self.x[side][c] + self.y[((0, 1), (4, 3))[side][c]])

        def forward(self, side, c):
            recv(self.x[1 - side][c][:2])
            start(self.corner[side][c])

        def finish(self, side, c):
            recv(self.x[1 - side][c][2:] + self.corner[side][c])

    def grouped(items, which, act):
        groups = {}
        for item in items:
            groups.setdefault(id(item[which]), []).append(item)
        for group in groups.values():
            @pl.when(group[0][which])
            def _(group=group):
                for item in group:
                    act(item[0])

    def start(items):
        grouped(items, 1, lambda c: c.start())

    def recv(items):
        grouped(items, 2, lambda c: c.wait_recv())

    def sent(items):
        grouped(items, 1, lambda c: c.wait_send())

    def conv_y(buf, band_ref, yf, order, lo, hi):
        def pair(p, carry):
            x = 2 * p
            for ch, fields in order:
                columns = []
                for j in range(2):
                    h, l = split(buf[ch, x + j])
                    columns.append(jnp.concatenate([h, l, h, h[:16]], 0))
                rhs = jnp.concatenate(columns, 1)
                out = jnp.dot(band_ref[ch], rhs, preferred_element_type=F32)
                for q, f in enumerate(fields):
                    for j in range(2):
                        yf[f, x + j] = out[q * COLS : (q + 1) * COLS, j * DEPTH : (j + 1) * DEPTH]
            return carry

        lax.fori_loop(lo, hi, pair, 0, unroll=2)

    def decaying(rows, n):
        q, q9 = DECAY, DECAY**9
        ahead, behind = [None] * n, [None] * n
        acc = rows[-8]
        for k in range(-7, 1):
            acc = acc * q + rows[k]
        behind[0] = acc
        for x in range(1, n):
            acc = acc * q + (rows[x] - q9 * rows[x - 9])
            behind[x] = acc
        acc = rows[n + 7]
        for k in range(n + 6, n - 1, -1):
            acc = acc * q + rows[k]
        acc = acc * q
        ahead[n - 1] = acc
        for x in range(n - 2, -1, -1):
            acc = (acc + rows[x + 1]) * q - q9 * rows[x + 9]
            ahead[x] = acc
        return [a + b for a, b in zip(ahead, behind)]

    def conv_x(r0, n, yf, specs):
        def chunk(j, carry):
            cols = pl.ds(pl.multiple_of(j * 16, 16), 16)
            for f, taps, radius, kind, comp in specs:
                rows = {i: yf[f, r0 + W + i, cols, :] for i in range(-radius, n + radius)}
                if taps is None:
                    outs = decaying(rows, n)
                else:
                    outs = []
                    for x in range(n):
                        acc = None
                        for k in range(radius + 1):
                            w = taps[8 + k]
                            if w == 0.0:
                                continue
                            v = rows[x] if k == 0 else rows[x + k] + rows[x - k]
                            acc = w * v if acc is None else acc + w * v
                        outs.append(acc)
                for x in range(n):
                    h, l = split(outs[x])
                    at = pl.ds(pl.multiple_of(x * COLS + j * 16, 16), 16)
                    lh[kind, comp, at, pl.ds(0, DEPTH)] = h
                    lh[kind, comp, at, pl.ds(DEPTH, DEPTH)] = l
            return carry

        lax.fori_loop(0, COLS // 16, chunk, 0)

    def conv_z(kind, comp, n, table):
        v = jnp.dot(lh[kind, comp, pl.ds(0, n * COLS)], table, preferred_element_type=F32)
        return v if v.shape[1] == DEPTH else v[:, :DEPTH] + v[:, DEPTH:]

    specs_a = []
    for c, r in ((0, 5), (1, 7)):
        specs_a.append((c * 3 + 0, x_taps(0, c, SEGMENTS[c]), r, 0, c))
        specs_a.append((c * 3 + 1, x_taps(1, c), r, 1, c))
        specs_a.append((c * 3 + 2, None, 8, 2, c))
    specs_b = []
    for c, r in ((0, 5), (1, 7)):
        specs_b.append((2 + c, x_taps(0, c, SEGMENTS[c]), r, 0, c))
        specs_b.append((c, x_taps(1, c), r, 1, c))

    def convs_a(it, r0, n):
        conv_x(r0, n, yfa, specs_a)
        at = pl.ds(r0 * COLS, n * COLS)
        for c in range(2):
            lanes = pl.ds(c * DEPTH, DEPTH)
            cres[it, 0, at, lanes] = conv_z(0, c, n, zp_ref[c])
            cres[it, 1, at, lanes] = conv_z(1, c, n, zs_ref[c])
            cres[it, 2, at, lanes] = conv_z(2, c, n, za_ref[...])

    def derive(it, r0, n, der):
        def row(x, carry):
            at = pl.ds(pl.multiple_of(x * COLS, COLS), COLS)

            def both(kind):
                out = []
                for c in range(2):
                    lanes = pl.ds(c * DEPTH, DEPTH)
                    v = cres[0, kind, at, lanes]
                    if it == 1:
                        v = (1.0 - DAMPING) * v + scl[c, 0:1] * cres[1, kind, at, lanes]
                    out.append(v)
                return out

            p0, p1 = both(0)
            s0, s1 = both(1)
            a0, a1 = both(2)
            t = 1.0 + (p0 + p1)
            n2 = s0 + s1
            der[0, x + W, pl.ds(W, COLS), :] = jnp.log(t) + (2.0 * CROSS) * n2 * t
            der[1, x + W, pl.ds(W, COLS), :] = n2 / t + CROSS * n2 * n2
            for i in range(2):
                att[i, at] = ATTRACT[i][0] * a0 + ATTRACT[i][1] * a1
            return carry

        lax.fori_loop(r0, r0 + n, row, 0)

    def stage_a(it, r0, n, der):
        convs_a(it, r0, n)
        derive(it, r0, n, der)

    def stage_b(r0, n, dest, off):
        conv_x(r0, n, yfb, specs_b)
        for i in range(2):
            res[i, pl.ds(0, n * COLS)] = conv_z(0, i, n, zp_ref[i]) + conv_z(1, i, n, zs_ref[i])

        def row(x, carry):
            at = pl.ds(pl.multiple_of(x * COLS, COLS), COLS)
            glob = pl.ds(pl.multiple_of((r0 + x) * COLS, COLS), COLS)
            keep = mask[r0 + x] == 0
            for i in range(2):
                v = jnp.where(keep, jnp.exp(att[i, glob] - res[i, at]), 0.0)
                dest[i, r0 + x + off, pl.ds(off, COLS), :] = v
                part = v[0:8]
                for q in range(1, COLS // 8):
                    part = part + v[8 * q : 8 * q + 8]
                tot[i] = tot[i] + part
            return carry

        lax.fori_loop(0, n, row, 0)

    copies = []

    def sum_start(it, s, mine):
        arbuf[it, s] = mine
        out = []
        for d, peer in enumerate(stages[s]):
            c = pltpu.make_async_remote_copy(
                src_ref=arbuf.at[it, s],
                dst_ref=arrecv.at[it, s, d],
                send_sem=as_.at[it, s, d],
                recv_sem=ar_.at[it, s, d],
                device_id=peer,
                device_id_type=MESH,
            )
            c.start()
            out.append(c)
        copies.extend(out)
        return out

    def sum_finish(it, s, mine, out):
        for d, c in enumerate(out):
            c.wait_recv()
            mine = mine + arrecv[it, s, d]
        return mine

    def local_total():
        sums = [jnp.sum(tot[i], axis=0, keepdims=True) for i in range(2)]
        rowid = lax.broadcasted_iota(jnp.int32, (8, DEPTH), 0)
        return jnp.where(rowid == 0, sums[0], jnp.where(rowid == 1, sums[1], 0.0))

    def scales(mine, dest):
        total = jnp.sum(mine, axis=1, keepdims=True)
        for i in range(2):
            dest[i] = jnp.broadcast_to(DAMPING * load_ref[i] * cells / total[i : i + 1], (8, DEPTH))

    order_a = ((0, (0, 1, 2)), (1, (3, 4, 5)))
    order_b = ((0, (0, 1)), (1, (2, 3)))
    x_rho = Exchange(0, rho, W)
    x_der1 = Exchange(1, der1, W - 1)
    x_prp = Exchange(2, prp, W)
    x_der2 = Exchange(3, der2, W - 1)
    pairs = (((2, 4), (0, 2)), ((20, 22), (22, 24)))
    first = ((0, HALF), (ROWS - HALF, ROWS - 2 * HALF))
    sides = (0, 1)

    for c in (NEAR, FAR):
        for side in sides:
            x_rho.send(side, c)
    start(x_rho.y[2])
    for buf in (der1, prp, der2):
        zeros(buf)
    tot[...] = jnp.zeros_like(tot)
    tables[0].wait()
    recv(sum(x_rho.y, []))
    conv_y(rho, ya_ref, yfa, order_a, 4, 12)
    for side in sides:
        x_rho.forward(side, NEAR)
    conv_y(rho, ya_ref, yfa, order_a, 12, 20)
    for t in tables[1:4]:
        t.wait()
    stage_a(0, 8, 8, der1)
    for side in sides:
        x_rho.forward(side, FAR)
    stage_a(0, 16, 8, der1)
    start(x_der1.y[2])
    for side in sides:
        x_rho.finish(side, NEAR)
        conv_y(rho, ya_ref, yfa, order_a, *pairs[side][NEAR])
        stage_a(0, first[side][FAR], HALF, der1)
        x_der1.send(side, FAR)
    for side in sides:
        x_rho.finish(side, FAR)
        conv_y(rho, ya_ref, yfa, order_a, *pairs[side][FAR])
        stage_a(0, first[side][NEAR], HALF, der1)
        x_der1.send(side, NEAR)

    def proposals(x_der, der, dest, off, between, after):
        recv(x_der.y[2])
        conv_y(der, yb_ref, yfb, order_b, 8, 16)
        for side in sides:
            x_der.forward(side, FAR)
        recv(x_der.y[1])
        conv_y(der, yb_ref, yfb, order_b, 6, 8)
        recv(x_der.y[3])
        conv_y(der, yb_ref, yfb, order_b, 16, 18)
        recv(x_der.y[0])
        conv_y(der, yb_ref, yfb, order_b, 4, 6)
        recv(x_der.y[4])
        conv_y(der, yb_ref, yfb, order_b, 18, 20)
        stage_b(8, 8, dest, off)
        for side in sides:
            x_der.forward(side, NEAR)
        stage_b(16, 8, dest, off)
        between()
        for side in sides:
            x_der.finish(side, FAR)
            conv_y(der, yb_ref, yfb, order_b, *pairs[side][FAR])
        for side in sides:
            x_der.finish(side, NEAR)
            conv_y(der, yb_ref, yfb, order_b, *pairs[side][NEAR])
            stage_b(first[side][NEAR], HALF, dest, off)
            after(side, NEAR)
        for side in sides:
            stage_b(first[side][FAR], HALF, dest, off)
            after(side, FAR)

    for t in tables[4:]:
        t.wait()
    proposals(x_der1, der1, prp, W, lambda: start(x_prp.y[2]), x_prp.send)

    mine = local_total()
    tot[...] = jnp.zeros_like(tot)
    out = sum_start(0, 0, mine)
    recv(x_prp.y[2])
    conv_y(prp, ya_ref, yfa, order_a, 8, 16)
    recv(x_prp.y[0] + x_prp.y[4] + x_prp.y[1] + x_prp.y[3])
    conv_y(prp, ya_ref, yfa, order_a, 4, 8)
    for side in sides:
        x_prp.forward(side, NEAR)
    conv_y(prp, ya_ref, yfa, order_a, 16, 20)
    mine = sum_finish(0, 0, mine, out)
    out = sum_start(0, 1, mine)
    convs_a(1, 8, 8)
    for side in sides:
        x_prp.forward(side, FAR)
    convs_a(1, 16, 8)
    for side in sides:
        x_prp.finish(side, NEAR)
        conv_y(prp, ya_ref, yfa, order_a, *pairs[side][NEAR])
        convs_a(1, first[side][FAR], HALF)
    mine = sum_finish(0, 1, mine, out)
    scales(mine, scl)
    for side in sides:
        derive(1, first[side][FAR], HALF, der2)
        x_der2.send(side, FAR)
    derive(1, 8, 16, der2)
    start(x_der2.y[2])
    for side in sides:
        x_prp.finish(side, FAR)
        conv_y(prp, ya_ref, yfa, order_a, *pairs[side][FAR])
        convs_a(1, first[side][NEAR], HALF)
        derive(1, first[side][NEAR], HALF, der2)
        x_der2.send(side, NEAR)

    def base():
        def row(x, carry):
            for c in range(2):
                new = (1.0 - DAMPING) * rho[c, x + W, pl.ds(W, COLS), :] + scl[c, 0:1] * prp[
                    c, x + W, pl.ds(W, COLS), :
                ]
                base_ref[c, x] = (1.0 - DAMPING) * new
            return carry

        lax.fori_loop(0, ROWS, row, 0)

    proposals(x_der2, der2, prop_ref, 0, base, lambda side, c: None)
    mine = local_total()
    out = sum_start(1, 0, mine)
    sent(x_rho.all + x_der1.all + x_prp.all + x_der2.all)
    mine = sum_finish(1, 0, mine, out)
    out = sum_start(1, 1, mine)
    for c in copies[: -len(out)]:
        c.wait_send()
    mine = sum_finish(1, 1, mine, out)
    scales(mine, scl_ref)
    for c in out:
        c.wait_send()


def last_kernel(base_ref, prop_ref, scl_ref, out_hbm, buf, sem):
    step = 8
    copies = []
    for x in range(0, ROWS, step):

        def row(i, carry):
            for c in range(2):
                buf[c, i] = base_ref[c, i] + scl_ref[c, 0:1] * prop_ref[c, i]
            return carry

        lax.fori_loop(x, x + step, row, 0)
        at = pl.ds(x, step)
        c = pltpu.make_async_copy(buf.at[:, at], out_hbm.at[:, at], sem.at[x // step])
        c.start()
        copies.append(c)
    for c in copies:
        c.wait()


def body(density_init, solid_mask, loadings):
    consts = [jnp.asarray(c) for c in constants()]
    anyspace = pl.BlockSpec(memory_space=pl.ANY)
    vmem = pl.BlockSpec(memory_space=pltpu.VMEM)
    smem = pl.BlockSpec(memory_space=pltpu.SMEM)
    padded = pltpu.VMEM((2, PR, PC, DEPTH), F32)
    field = pltpu.VMEM((2, ROWS, COLS, DEPTH), F32)
    dma = pltpu.SemaphoreType.DMA
    base, prop, scl = pl.pallas_call(
        kernel,
        out_shape=(field, field, pltpu.VMEM((2, 8, DEPTH), F32)),
        in_specs=[anyspace, anyspace, smem] + [anyspace] * len(consts),
        out_specs=(vmem, vmem, vmem),
        scratch_shapes=[
            padded, padded, padded, padded,
            pltpu.VMEM((ROWS, COLS, DEPTH), jnp.int32),
            pltpu.VMEM((6, PR, COLS, DEPTH), F32),
            pltpu.VMEM((4, PR, COLS, DEPTH), F32),
            pltpu.VMEM((3, 2, BLK * COLS, 2 * DEPTH), BF16),
            pltpu.VMEM((2, BLK * COLS, DEPTH), F32),
            pltpu.VMEM((2, 3, ROWS * COLS, 2 * DEPTH), F32),
            pltpu.VMEM((2, ROWS * COLS, DEPTH), F32),
            pltpu.VMEM((2, 8, DEPTH), F32),
            pltpu.VMEM((2, 8, DEPTH), F32),
            pltpu.VMEM((2, 2, 8, DEPTH), F32),
            pltpu.VMEM((2, 2, 15, 8, DEPTH), F32),
        ]
        + [pltpu.VMEM(c.shape, BF16) for c in consts]
        + [dma((8,)), dma((4, 32)), dma((4, 32)), dma((2, 2, 15)), dma((2, 2, 15))],
        compiler_params=pltpu.CompilerParams(
            collective_id=0, has_side_effects=True, vmem_limit_bytes=54 * 2**20
        ),
        name="picard",
    )(density_init, solid_mask, loadings, *consts)
    return pl.pallas_call(
        last_kernel,
        out_shape=jax.ShapeDtypeStruct((2, ROWS, COLS, DEPTH), F32),
        in_specs=[vmem, vmem, vmem],
        out_specs=anyspace,
        scratch_shapes=[field, dma((4,))],
        compiler_params=pltpu.CompilerParams(vmem_limit_bytes=4 * 2**20),
        name="last",
    )(base, prop, scl)


def solution(mesh):
    in_specs = (P(None, "gx", "gy", None), P("gx", "gy", None), P())
    out_specs = P(None, "gx", "gy", None)
    return jax.shard_map(body, mesh=mesh, in_specs=in_specs, out_specs=out_specs, check_vma=False)
```

```python
import jax
import jax.numpy as jnp
import ml_dtypes
import numpy as np
from jax import lax
from jax.experimental import pallas as pl
from jax.experimental.pallas import tpu as pltpu
from jax.sharding import PartitionSpec as P

SEGMENTS = (1.5131, 1.0)
RADII = (6.0, 8.0)
CROSS = 0.25
DAMPING = 0.3
ATTRACT = ((0.3, 0.22), (0.22, 0.16))

W = 8
ROWS, COLS, DEPTH = 32, 64, 128
PR, PC = ROWS + 2 * W, COLS + 2 * W
BLK = 8
GX, GY, NZ_, NY_ = 32, 8, 8, 4
NEAR, FAR = 0, 1
HALF = 4
DECAY = float(np.exp(-0.25))
MESH = pl.DeviceIdType.MESH
BF16 = jnp.bfloat16
F32 = jnp.float32


def raw_profile(kind, radius):
    k = np.arange(17) - 8.0
    if kind == 0:
        return np.maximum(radius * radius - k * k, 0.0)
    if kind == 1:
        return k * k * np.maximum(radius * radius - k * k, 0.0)
    v = np.exp(-np.abs(k) / 4.0)
    return v / v.sum()


RAW = {(k, c): raw_profile(k, RADII[c]) for k in range(3) for c in range(2)}


def x_taps(kind, comp, extra=1.0):
    v = RAW[kind, comp]
    return (v / v.sum() ** 3 * extra).tolist()


def split_np(table):
    hi = table.astype(np.float32).astype(ml_dtypes.bfloat16)
    lo = (table - hi.astype(np.float64)).astype(np.float32).astype(ml_dtypes.bfloat16)
    return hi, lo


def band_y(profiles):
    tables = []
    for taps in profiles:
        t = np.zeros((COLS, PC))
        for o in range(COLS):
            t[o, o : o + 17] = taps
        tables.append(t)
    hi, lo = split_np(np.concatenate(tables, 0))
    pad = np.zeros((hi.shape[0], 16), ml_dtypes.bfloat16)
    return np.concatenate([hi, hi, lo, pad], 1)


def band_z(taps):
    t = np.zeros((DEPTH, DEPTH))
    for o in range(DEPTH):
        for k in range(17):
            i = o + k - 8
            if 0 <= i < DEPTH:
                t[i, o] = taps[k]
    return t


def wide_z(table):
    hi, lo = split_np(table)
    return np.concatenate(
        [np.concatenate([hi, lo], 1), np.concatenate([hi, np.zeros_like(lo)], 1)], 0
    )


def constants():
    ya = [band_y([RAW[0, c], RAW[1, c], RAW[2, c]]) for c in range(2)]
    yb = [band_y([RAW[k, 0], RAW[k, 1]]) for k in (1, 0)]
    zp = [np.concatenate([split_np(band_z(RAW[0, c]))[0]] * 2, 0) for c in range(2)]
    zs = [wide_z(band_z(RAW[1, c])) for c in range(2)]
    za = wide_z(band_z(RAW[2, 0]) * RAW[2, 0][8])
    return [np.stack(ya), np.stack(yb), np.stack(zp), np.stack(zs), za]


def split(v):
    hi = v.astype(BF16)
    return hi, (v - hi.astype(F32)).astype(BF16)


def kernel(
    dens_hbm, mask_hbm, load_ref, ya_hbm, yb_hbm, zp_hbm, zs_hbm, za_hbm,
    base_ref, prop_ref, scl_ref,
    rho, prp, der1, der2, mask, yfa, yfb, lh, res, cres, att, tot, scl, arbuf, arrecv,
    ya_ref, yb_ref, zp_ref, zs_ref, za_ref,
    in_sem, hs, hr, as_, ar_,
):
    gx, gy = lax.axis_index("gx"), lax.axis_index("gy")
    yy, zz = gx // NZ_, gx % NZ_
    cells = float(ROWS * GX * COLS * GY * DEPTH)

    loads = [
        pltpu.make_async_copy(
            dens_hbm, rho.at[:, pl.ds(W, ROWS), pl.ds(W, COLS), :], in_sem.at[0]
        ),
        pltpu.make_async_copy(mask_hbm, mask, in_sem.at[1]),
    ]
    wanted = (
        (ya_hbm, ya_ref), (zp_hbm, zp_ref), (zs_hbm, zs_ref), (za_hbm, za_ref), (yb_hbm, yb_ref),
    )
    tables = [
        pltpu.make_async_copy(a, b, in_sem.at[2 + i]) for i, (a, b) in enumerate(wanted)
    ]
    for c in loads + tables:
        c.start()

    xx, core = gy // 2, gy % 2
    plane = [(dy, dx) for dy in range(NY_) for dx in range(4) if (dy, dx) != (0, 0)]
    plane.sort(key=lambda p: -(min(p[0], NY_ - p[0]) + min(p[1], 4 - p[1])))
    line = [(dz, dc) for dz in range(NZ_) for dc in range(2) if (dz, dc) != (0, 0)]
    line.sort(key=lambda p: -(2 * min(p[0], NZ_ - p[0]) + p[1]))
    stages = [
        [(((yy + dy) % NY_) * NZ_ + zz, ((xx + dx) % 4) * 2 + core) for dy, dx in plane],
        [(yy * NZ_ + (zz + dz) % NZ_, xx * 2 + (core + dc) % 2) for dz, dc in line],
    ]
    barrier = pltpu.get_barrier_semaphore()
    greeted = 0
    for peers in stages:
        for peer in peers:
            greeted += 1
            pl.semaphore_signal(barrier, inc=1, device_id=peer, device_id_type=MESH)

    has_lo, has_hi = gx > 0, gx < GX - 1
    has_l, has_r = gy > 0, gy < GY - 1

    near = (
        (has_lo, (gx - 1, gy)),
        (has_hi, (gx + 1, gy)),
        (has_l, (gx, gy - 1)),
        (has_r, (gx, gy + 1)),
    )
    for there, peer in near:
        @pl.when(there)
        def _(peer=peer):
            pl.semaphore_signal(barrier, inc=1, device_id=peer, device_id_type=MESH)

    def zeros(buf):
        @pl.when(gx == 0)
        def _():
            buf[:, pl.ds(0, W)] = jnp.zeros((2, W, PC, DEPTH), F32)

        @pl.when(gx == GX - 1)
        def _():
            buf[:, pl.ds(W + ROWS, W)] = jnp.zeros((2, W, PC, DEPTH), F32)

        @pl.when(gy == 0)
        def _():
            buf[:, :, pl.ds(0, W)] = jnp.zeros((2, PR, W, DEPTH), F32)

        @pl.when(gy == GY - 1)
        def _():
            buf[:, :, pl.ds(W + COLS, W)] = jnp.zeros((2, PR, W, DEPTH), F32)

    zeros(rho)
    for c in loads:
        c.wait()

    def mask_row(x, carry):
        keep = mask[x] == 0
        for c in range(2):
            v = rho[c, x + W, pl.ds(W, COLS), :]
            rho[c, x + W, pl.ds(W, COLS), :] = jnp.where(keep, v, 0.0)
        return carry

    lax.fori_loop(0, ROWS, mask_row, 0)

    pl.semaphore_wait(
        barrier, greeted + sum(there.astype(jnp.int32) for there, _ in near)
    )

    with_both = [(x & has_l, x & has_r) for x in (has_lo, has_hi)]

    class Exchange:
        def __init__(self, n, buf, w):
            count = [0]

            def item(src, dst, peer, to, frm):
                k = count[0]
                count[0] += 1
                c = pltpu.make_async_remote_copy(
                    src_ref=buf.at[(slice(None),) + src],
                    dst_ref=buf.at[(slice(None),) + dst],
                    send_sem=hs.at[n, k],
                    recv_sem=hr.at[n, k],
                    device_id=peer,
                    device_id_type=MESH,
                )
                return c, to, frm

            down, up = (gx - 1, gy), (gx + 1, gy)
            left, right = (gx, gy - 1), (gx, gy + 1)
            l_src, r_src = pl.ds(W, W), pl.ds(COLS, W)
            l_dst, r_dst = pl.ds(0, W), pl.ds(W + COLS, W)
            parts = (l_src, r_src, pl.ds(2 * W, COLS - 2 * W))
            lo_rows = ((0, HALF), (HALF, w - HALF))
            hi_rows = ((ROWS - HALF, HALF), (ROWS - w, w - HALF))
            self.x = [[], []]
            self.corner = [[], []]
            for r, k in lo_rows:
                src, dst = pl.ds(W + r, k), pl.ds(W + ROWS + r, k)
                self.x[0].append([item((src, p), (dst, p), down, has_lo, has_hi) for p in parts])
            for r, k in hi_rows:
                src, dst = pl.ds(W + r, k), pl.ds(W + r - ROWS, k)
                self.x[1].append([item((src, p), (dst, p), up, has_hi, has_lo) for p in parts])
            for side, rows, shift in ((0, hi_rows, -ROWS), (1, lo_rows, ROWS)):
                with_l, with_r = with_both[side]
                for r, k in rows:
                    at = pl.ds(W + r + shift, k)
                    self.corner[side].append(
                        [
                            item((at, l_src), (at, r_dst), left, with_l, with_r),
                            item((at, r_src), (at, l_dst), right, with_r, with_l),
                        ]
                    )
            self.y = []
            for r, k in ((0, 4), (4, 4), (8, 16), (24, 4), (28, 4)):
                at = pl.ds(W + r, k)
                self.y.append(
                    [
                        item((at, l_src), (at, r_dst), left, has_l, has_r),
                        item((at, r_src), (at, l_dst), right, has_r, has_l),
                    ]
                )
            self.all = sum(self.x[0] + self.x[1] + self.corner[0] + self.corner[1] + self.y, [])

        def send(self, side, c):
            start(self.x[side][c] + self.y[((0, 1), (4, 3))[side][c]])

        def forward(self, side, c):
            recv(self.x[1 - side][c][:2])
            start(self.corner[side][c])

        def finish(self, side, c):
            recv(self.x[1 - side][c][2:] + self.corner[side][c])

    def grouped(items, which, act):
        groups = {}
        for item in items:
            groups.setdefault(id(item[which]), []).append(item)
        for group in groups.values():
            @pl.when(group[0][which])
            def _(group=group):
                for item in group:
                    act(item[0])

    def start(items):
        grouped(items, 1, lambda c: c.start())

    def recv(items):
        grouped(items, 2, lambda c: c.wait_recv())

    def sent(items):
        grouped(items, 1, lambda c: c.wait_send())

    def conv_y(buf, band_ref, yf, order, lo, hi):
        def pair(p, carry):
            x = 2 * p
            for ch, fields in order:
                columns = []
                for j in range(2):
                    h, l = split(buf[ch, x + j])
                    columns.append(jnp.concatenate([h, l, h, h[:16]], 0))
                rhs = jnp.concatenate(columns, 1)
                out = jnp.dot(band_ref[ch], rhs, preferred_element_type=F32)
                for q, f in enumerate(fields):
                    for j in range(2):
                        yf[f, x + j] = out[q * COLS : (q + 1) * COLS, j * DEPTH : (j + 1) * DEPTH]
            return carry

        lax.fori_loop(lo, hi, pair, 0, unroll=2)

    def decaying(rows, n):
        q, q9 = DECAY, DECAY**9
        ahead, behind = [None] * n, [None] * n
        acc = rows[-8]
        for k in range(-7, 1):
            acc = acc * q + rows[k]
        behind[0] = acc
        for x in range(1, n):
            acc = acc * q + (rows[x] - q9 * rows[x - 9])
            behind[x] = acc
        acc = rows[n + 7]
        for k in range(n + 6, n - 1, -1):
            acc = acc * q + rows[k]
        acc = acc * q
        ahead[n - 1] = acc
        for x in range(n - 2, -1, -1):
            acc = (acc + rows[x + 1]) * q - q9 * rows[x + 9]
            ahead[x] = acc
        return [a + b for a, b in zip(ahead, behind)]

    def conv_x(r0, n, yf, specs):
        def chunk(j, carry):
            cols = pl.ds(pl.multiple_of(j * 16, 16), 16)
            for f, taps, radius, kind, comp in specs:
                rows = {i: yf[f, r0 + W + i, cols, :] for i in range(-radius, n + radius)}
                if taps is None:
                    outs = decaying(rows, n)
                else:
                    outs = []
                    for x in range(n):
                        acc = None
                        for k in range(radius + 1):
                            w = taps[8 + k]
                            if w == 0.0:
                                continue
                            v = rows[x] if k == 0 else rows[x + k] + rows[x - k]
                            acc = w * v if acc is None else acc + w * v
                        outs.append(acc)
                for x in range(n):
                    h, l = split(outs[x])
                    at = pl.ds(pl.multiple_of(x * COLS + j * 16, 16), 16)
                    lh[kind, comp, at, pl.ds(0, DEPTH)] = h
                    lh[kind, comp, at, pl.ds(DEPTH, DEPTH)] = l
            return carry

        lax.fori_loop(0, COLS // 16, chunk, 0)

    def conv_z(kind, comp, n, table):
        v = jnp.dot(lh[kind, comp, pl.ds(0, n * COLS)], table, preferred_element_type=F32)
        return v if v.shape[1] == DEPTH else v[:, :DEPTH] + v[:, DEPTH:]

    specs_a = []
    for c, r in ((0, 5), (1, 7)):
        specs_a.append((c * 3 + 0, x_taps(0, c, SEGMENTS[c]), r, 0, c))
        specs_a.append((c * 3 + 1, x_taps(1, c), r, 1, c))
        specs_a.append((c * 3 + 2, None, 8, 2, c))
    specs_b = []
    for c, r in ((0, 5), (1, 7)):
        specs_b.append((2 + c, x_taps(0, c, SEGMENTS[c]), r, 0, c))
        specs_b.append((c, x_taps(1, c), r, 1, c))

    def convs_a(it, r0, n):
        conv_x(r0, n, yfa, specs_a)
        at = pl.ds(r0 * COLS, n * COLS)
        for c in range(2):
            lanes = pl.ds(c * DEPTH, DEPTH)
            cres[it, 0, at, lanes] = conv_z(0, c, n, zp_ref[c])
            cres[it, 1, at, lanes] = conv_z(1, c, n, zs_ref[c])
            cres[it, 2, at, lanes] = conv_z(2, c, n, za_ref[...])

    def derive(it, r0, n, der):
        def row(x, carry):
            at = pl.ds(pl.multiple_of(x * COLS, COLS), COLS)

            def both(kind):
                out = []
                for c in range(2):
                    lanes = pl.ds(c * DEPTH, DEPTH)
                    v = cres[0, kind, at, lanes]
                    if it == 1:
                        v = (1.0 - DAMPING) * v + scl[c, 0:1] * cres[1, kind, at, lanes]
                    out.append(v)
                return out

            p0, p1 = both(0)
            s0, s1 = both(1)
            a0, a1 = both(2)
            t = 1.0 + (p0 + p1)
            n2 = s0 + s1
            der[0, x + W, pl.ds(W, COLS), :] = jnp.log(t) + (2.0 * CROSS) * n2 * t
            der[1, x + W, pl.ds(W, COLS), :] = n2 / t + CROSS * n2 * n2
            for i in range(2):
                att[i, at] = ATTRACT[i][0] * a0 + ATTRACT[i][1] * a1
            return carry

        lax.fori_loop(r0, r0 + n, row, 0)

    def stage_a(it, r0, n, der):
        convs_a(it, r0, n)
        derive(it, r0, n, der)

    def stage_b(r0, n, dest, off):
        conv_x(r0, n, yfb, specs_b)
        for i in range(2):
            res[i, pl.ds(0, n * COLS)] = conv_z(0, i, n, zp_ref[i]) + conv_z(1, i, n, zs_ref[i])

        def row(x, carry):
            at = pl.ds(pl.multiple_of(x * COLS, COLS), COLS)
            glob = pl.ds(pl.multiple_of((r0 + x) * COLS, COLS), COLS)
            keep = mask[r0 + x] == 0
            for i in range(2):
                v = jnp.where(keep, jnp.exp(att[i, glob] - res[i, at]), 0.0)
                dest[i, r0 + x + off, pl.ds(off, COLS), :] = v
                part = v[0:8]
                for q in range(1, COLS // 8):
                    part = part + v[8 * q : 8 * q + 8]
                tot[i] = tot[i] + part
            return carry

        lax.fori_loop(0, n, row, 0)

    copies = []

    def sum_start(it, s, mine):
        arbuf[it, s] = mine
        out = []
        for d, peer in enumerate(stages[s]):
            c = pltpu.make_async_remote_copy(
                src_ref=arbuf.at[it, s],
                dst_ref=arrecv.at[it, s, d],
                send_sem=as_.at[it, s, d],
                recv_sem=ar_.at[it, s, d],
                device_id=peer,
                device_id_type=MESH,
            )
            c.start()
            out.append(c)
        copies.extend(out)
        return out

    def sum_finish(it, s, mine, out):
        for d in range(len(out) - 1, -1, -1):
            out[d].wait_recv()
            mine = mine + arrecv[it, s, d]
        return mine

    def local_total():
        sums = [jnp.sum(tot[i], axis=0, keepdims=True) for i in range(2)]
        rowid = lax.broadcasted_iota(jnp.int32, (8, DEPTH), 0)
        return jnp.where(rowid == 0, sums[0], jnp.where(rowid == 1, sums[1], 0.0))

    def scales(mine, dest):
        total = jnp.sum(mine, axis=1, keepdims=True)
        for i in range(2):
            dest[i] = jnp.broadcast_to(DAMPING * load_ref[i] * cells / total[i : i + 1], (8, DEPTH))

    order_a = ((0, (0, 1, 2)), (1, (3, 4, 5)))
    order_b = ((0, (0, 1)), (1, (2, 3)))
    x_rho = Exchange(0, rho, W)
    x_der1 = Exchange(1, der1, W - 1)
    x_prp = Exchange(2, prp, W)
    x_der2 = Exchange(3, der2, W - 1)
    pairs = (((2, 4), (0, 2)), ((20, 22), (22, 24)))
    first = ((0, HALF), (ROWS - HALF, ROWS - 2 * HALF))
    sides = (0, 1)

    for c in (NEAR, FAR):
        for side in sides:
            x_rho.send(side, c)
    start(x_rho.y[2])
    for buf in (der1, prp, der2):
        zeros(buf)
    tot[...] = jnp.zeros_like(tot)
    tables[0].wait()
    recv(sum(x_rho.y, []))
    conv_y(rho, ya_ref, yfa, order_a, 4, 12)
    for side in sides:
        x_rho.forward(side, NEAR)
    conv_y(rho, ya_ref, yfa, order_a, 12, 20)
    for t in tables[1:4]:
        t.wait()
    stage_a(0, 8, 8, der1)
    for side in sides:
        x_rho.forward(side, FAR)
    stage_a(0, 16, 8, der1)
    start(x_der1.y[2])
    for side in sides:
        x_rho.finish(side, NEAR)
        conv_y(rho, ya_ref, yfa, order_a, *pairs[side][NEAR])
        stage_a(0, first[side][FAR], HALF, der1)
        x_der1.send(side, FAR)
    for side in sides:
        x_rho.finish(side, FAR)
        conv_y(rho, ya_ref, yfa, order_a, *pairs[side][FAR])
        stage_a(0, first[side][NEAR], HALF, der1)
        x_der1.send(side, NEAR)

    def proposals(x_der, der, dest, off, between, after):
        recv(x_der.y[2])
        conv_y(der, yb_ref, yfb, order_b, 8, 16)
        for side in sides:
            x_der.forward(side, FAR)
        recv(x_der.y[1])
        conv_y(der, yb_ref, yfb, order_b, 6, 8)
        recv(x_der.y[3])
        conv_y(der, yb_ref, yfb, order_b, 16, 18)
        recv(x_der.y[0])
        conv_y(der, yb_ref, yfb, order_b, 4, 6)
        recv(x_der.y[4])
        conv_y(der, yb_ref, yfb, order_b, 18, 20)
        stage_b(8, 8, dest, off)
        for side in sides:
            x_der.forward(side, NEAR)
        stage_b(16, 8, dest, off)
        between()
        for side in sides:
            x_der.finish(side, FAR)
            conv_y(der, yb_ref, yfb, order_b, *pairs[side][FAR])
        for side in sides:
            x_der.finish(side, NEAR)
            conv_y(der, yb_ref, yfb, order_b, *pairs[side][NEAR])
            stage_b(first[side][NEAR], HALF, dest, off)
            after(side, NEAR)
        for side in sides:
            stage_b(first[side][FAR], HALF, dest, off)
            after(side, FAR)

    for t in tables[4:]:
        t.wait()
    proposals(x_der1, der1, prp, W, lambda: start(x_prp.y[2]), x_prp.send)

    mine = local_total()
    tot[...] = jnp.zeros_like(tot)
    out = sum_start(0, 0, mine)
    recv(x_prp.y[2])
    conv_y(prp, ya_ref, yfa, order_a, 8, 16)
    recv(x_prp.y[0] + x_prp.y[4] + x_prp.y[1] + x_prp.y[3])
    conv_y(prp, ya_ref, yfa, order_a, 4, 8)
    for side in sides:
        x_prp.forward(side, NEAR)
    conv_y(prp, ya_ref, yfa, order_a, 16, 20)
    mine = sum_finish(0, 0, mine, out)
    out = sum_start(0, 1, mine)
    convs_a(1, 8, 8)
    for side in sides:
        x_prp.forward(side, FAR)
    convs_a(1, 16, 8)
    for side in sides:
        x_prp.finish(side, NEAR)
        conv_y(prp, ya_ref, yfa, order_a, *pairs[side][NEAR])
        convs_a(1, first[side][FAR], HALF)
    mine = sum_finish(0, 1, mine, out)
    scales(mine, scl)
    for side in sides:
        derive(1, first[side][FAR], HALF, der2)
        x_der2.send(side, FAR)
    derive(1, 8, 16, der2)
    start(x_der2.y[2])
    for side in sides:
        x_prp.finish(side, FAR)
        conv_y(prp, ya_ref, yfa, order_a, *pairs[side][FAR])
        convs_a(1, first[side][NEAR], HALF)
        derive(1, first[side][NEAR], HALF, der2)
        x_der2.send(side, NEAR)

    def base():
        def row(x, carry):
            for c in range(2):
                new = (1.0 - DAMPING) * rho[c, x + W, pl.ds(W, COLS), :] + scl[c, 0:1] * prp[
                    c, x + W, pl.ds(W, COLS), :
                ]
                base_ref[c, x] = (1.0 - DAMPING) * new
            return carry

        lax.fori_loop(0, ROWS, row, 0)

    proposals(x_der2, der2, prop_ref, 0, base, lambda side, c: None)
    mine = local_total()
    out = sum_start(1, 0, mine)
    sent(x_rho.all + x_der1.all + x_prp.all + x_der2.all)
    mine = sum_finish(1, 0, mine, out)
    out = sum_start(1, 1, mine)
    for c in copies[: -len(out)]:
        c.wait_send()
    mine = sum_finish(1, 1, mine, out)
    scales(mine, scl_ref)
    for c in out:
        c.wait_send()


def last_kernel(base_ref, prop_ref, scl_ref, out_hbm, buf, sem):
    step = 8
    copies = []
    for x in range(0, ROWS, step):

        def row(i, carry):
            for c in range(2):
                buf[c, i] = base_ref[c, i] + scl_ref[c, 0:1] * prop_ref[c, i]
            return carry

        lax.fori_loop(x, x + step, row, 0)
        at = pl.ds(x, step)
        c = pltpu.make_async_copy(buf.at[:, at], out_hbm.at[:, at], sem.at[x // step])
        c.start()
        copies.append(c)
    for c in copies:
        c.wait()


def body(density_init, solid_mask, loadings):
    consts = [jnp.asarray(c) for c in constants()]
    anyspace = pl.BlockSpec(memory_space=pl.ANY)
    vmem = pl.BlockSpec(memory_space=pltpu.VMEM)
    smem = pl.BlockSpec(memory_space=pltpu.SMEM)
    padded = pltpu.VMEM((2, PR, PC, DEPTH), F32)
    field = pltpu.VMEM((2, ROWS, COLS, DEPTH), F32)
    dma = pltpu.SemaphoreType.DMA
    base, prop, scl = pl.pallas_call(
        kernel,
        out_shape=(field, field, pltpu.VMEM((2, 8, DEPTH), F32)),
        in_specs=[anyspace, anyspace, smem] + [anyspace] * len(consts),
        out_specs=(vmem, vmem, vmem),
        scratch_shapes=[
            padded, padded, padded, padded,
            pltpu.VMEM((ROWS, COLS, DEPTH), jnp.int32),
            pltpu.VMEM((6, PR, COLS, DEPTH), F32),
            pltpu.VMEM((4, PR, COLS, DEPTH), F32),
            pltpu.VMEM((3, 2, BLK * COLS, 2 * DEPTH), BF16),
            pltpu.VMEM((2, BLK * COLS, DEPTH), F32),
            pltpu.VMEM((2, 3, ROWS * COLS, 2 * DEPTH), F32),
            pltpu.VMEM((2, ROWS * COLS, DEPTH), F32),
            pltpu.VMEM((2, 8, DEPTH), F32),
            pltpu.VMEM((2, 8, DEPTH), F32),
            pltpu.VMEM((2, 2, 8, DEPTH), F32),
            pltpu.VMEM((2, 2, 15, 8, DEPTH), F32),
        ]
        + [pltpu.VMEM(c.shape, BF16) for c in consts]
        + [dma((8,)), dma((4, 32)), dma((4, 32)), dma((2, 2, 15)), dma((2, 2, 15))],
        compiler_params=pltpu.CompilerParams(
            collective_id=0, has_side_effects=True, vmem_limit_bytes=54 * 2**20
        ),
        name="picard",
    )(density_init, solid_mask, loadings, *consts)
    return pl.pallas_call(
        last_kernel,
        out_shape=jax.ShapeDtypeStruct((2, ROWS, COLS, DEPTH), F32),
        in_specs=[vmem, vmem, vmem],
        out_specs=anyspace,
        scratch_shapes=[field, dma((4,))],
        compiler_params=pltpu.CompilerParams(vmem_limit_bytes=4 * 2**20),
        name="last",
    )(base, prop, scl)


def solution(mesh):
    in_specs = (P(None, "gx", "gy", None), P("gx", "gy", None), P())
    out_specs = P(None, "gx", "gy", None)
    return jax.shard_map(body, mesh=mesh, in_specs=in_specs, out_specs=out_specs, check_vma=False)
```

```python
import jax
import jax.numpy as jnp
import ml_dtypes
import numpy as np
from jax import lax
from jax.experimental import pallas as pl
from jax.experimental.pallas import tpu as pltpu
from jax.sharding import PartitionSpec as P

SEGMENTS = (1.5131, 1.0)
RADII = (6.0, 8.0)
CROSS = 0.25
DAMPING = 0.3
ATTRACT = ((0.3, 0.22), (0.22, 0.16))

W = 8
ROWS, COLS, DEPTH = 32, 64, 128
PR, PC = ROWS + 2 * W, COLS + 2 * W
BLK = 8
GX, GY, NZ_, NY_ = 32, 8, 8, 4
NEAR, FAR = 0, 1
HALF = 4
DECAY = float(np.exp(-0.25))
MESH = pl.DeviceIdType.MESH
BF16 = jnp.bfloat16
F32 = jnp.float32


def raw_profile(kind, radius):
    k = np.arange(17) - 8.0
    if kind == 0:
        return np.maximum(radius * radius - k * k, 0.0)
    if kind == 1:
        return k * k * np.maximum(radius * radius - k * k, 0.0)
    v = np.exp(-np.abs(k) / 4.0)
    return v / v.sum()


RAW = {(k, c): raw_profile(k, RADII[c]) for k in range(3) for c in range(2)}


def x_taps(kind, comp, extra=1.0):
    v = RAW[kind, comp]
    return (v / v.sum() ** 3 * extra).tolist()


def split_np(table):
    hi = table.astype(np.float32).astype(ml_dtypes.bfloat16)
    lo = (table - hi.astype(np.float64)).astype(np.float32).astype(ml_dtypes.bfloat16)
    return hi, lo


def band_y(profiles):
    tables = []
    for taps in profiles:
        t = np.zeros((COLS, PC))
        for o in range(COLS):
            t[o, o : o + 17] = taps
        tables.append(t)
    hi, lo = split_np(np.concatenate(tables, 0))
    pad = np.zeros((hi.shape[0], 16), ml_dtypes.bfloat16)
    return np.concatenate([hi, hi, lo, pad], 1)


def band_z(taps):
    t = np.zeros((DEPTH, DEPTH))
    for o in range(DEPTH):
        for k in range(17):
            i = o + k - 8
            if 0 <= i < DEPTH:
                t[i, o] = taps[k]
    return t


def wide_z(table):
    hi, lo = split_np(table)
    return np.concatenate(
        [np.concatenate([hi, lo], 1), np.concatenate([hi, np.zeros_like(lo)], 1)], 0
    )


def constants():
    ya = [band_y([RAW[0, c], RAW[1, c], RAW[2, c]]) for c in range(2)]
    yb = [band_y([RAW[k, 0], RAW[k, 1]]) for k in (1, 0)]
    zp = [np.concatenate([split_np(band_z(RAW[0, c]))[0]] * 2, 0) for c in range(2)]
    zs = [wide_z(band_z(RAW[1, c])) for c in range(2)]
    za = wide_z(band_z(RAW[2, 0]) * RAW[2, 0][8])
    return [np.stack(ya), np.stack(yb), np.stack(zp), np.stack(zs), za]


def split(v):
    hi = v.astype(BF16)
    return hi, (v - hi.astype(F32)).astype(BF16)


def kernel(
    dens_hbm, mask_hbm, load_ref, ya_hbm, yb_hbm, zp_hbm, zs_hbm, za_hbm,
    base_ref, prop_ref, scl_ref,
    rho, prp, der1, der2, mask, yfa, yfb, lh, res, cres, att, tot, scl, arbuf, arrecv,
    ya_ref, yb_ref, zp_ref, zs_ref, za_ref,
    in_sem, hs, hr, as_, ar_,
):
    gx, gy = lax.axis_index("gx"), lax.axis_index("gy")
    yy, zz = gx // NZ_, gx % NZ_
    cells = float(ROWS * GX * COLS * GY * DEPTH)

    loads = [
        pltpu.make_async_copy(
            dens_hbm, rho.at[:, pl.ds(W, ROWS), pl.ds(W, COLS), :], in_sem.at[0]
        ),
        pltpu.make_async_copy(mask_hbm, mask, in_sem.at[1]),
    ]
    wanted = (
        (ya_hbm, ya_ref), (zp_hbm, zp_ref), (zs_hbm, zs_ref), (za_hbm, za_ref), (yb_hbm, yb_ref),
    )
    tables = [
        pltpu.make_async_copy(a, b, in_sem.at[2 + i]) for i, (a, b) in enumerate(wanted)
    ]
    for c in loads + tables:
        c.start()

    xx, core = gy // 2, gy % 2
    plane = [(dy, dx) for dy in range(NY_) for dx in range(4) if (dy, dx) != (0, 0)]
    plane.sort(key=lambda p: -(min(p[0], NY_ - p[0]) + min(p[1], 4 - p[1])))
    line = [(dz, dc) for dz in range(NZ_) for dc in range(2) if (dz, dc) != (0, 0)]
    line.sort(key=lambda p: -(2 * min(p[0], NZ_ - p[0]) + p[1]))
    stages = [
        [(((yy + dy) % NY_) * NZ_ + zz, ((xx + dx) % 4) * 2 + core) for dy, dx in plane],
        [(yy * NZ_ + (zz + dz) % NZ_, xx * 2 + (core + dc) % 2) for dz, dc in line],
    ]
    barrier = pltpu.get_barrier_semaphore()
    greeted = 0
    for peers in stages:
        for peer in peers:
            greeted += 1
            pl.semaphore_signal(barrier, inc=1, device_id=peer, device_id_type=MESH)

    has_lo, has_hi = gx > 0, gx < GX - 1
    has_l, has_r = gy > 0, gy < GY - 1

    near = (
        (has_lo, (gx - 1, gy)),
        (has_hi, (gx + 1, gy)),
        (has_l, (gx, gy - 1)),
        (has_r, (gx, gy + 1)),
    )
    for there, peer in near:
        @pl.when(there)
        def _(peer=peer):
            pl.semaphore_signal(barrier, inc=1, device_id=peer, device_id_type=MESH)

    def zeros(buf):
        @pl.when(gx == 0)
        def _():
            buf[:, pl.ds(0, W)] = jnp.zeros((2, W, PC, DEPTH), F32)

        @pl.when(gx == GX - 1)
        def _():
            buf[:, pl.ds(W + ROWS, W)] = jnp.zeros((2, W, PC, DEPTH), F32)

        @pl.when(gy == 0)
        def _():
            buf[:, :, pl.ds(0, W)] = jnp.zeros((2, PR, W, DEPTH), F32)

        @pl.when(gy == GY - 1)
        def _():
            buf[:, :, pl.ds(W + COLS, W)] = jnp.zeros((2, PR, W, DEPTH), F32)

    zeros(rho)
    for c in loads:
        c.wait()

    def mask_row(x, carry):
        keep = mask[x] == 0
        for c in range(2):
            v = rho[c, x + W, pl.ds(W, COLS), :]
            rho[c, x + W, pl.ds(W, COLS), :] = jnp.where(keep, v, 0.0)
        return carry

    lax.fori_loop(0, ROWS, mask_row, 0)

    pl.semaphore_wait(
        barrier, greeted + sum(there.astype(jnp.int32) for there, _ in near)
    )

    with_both = [(x & has_l, x & has_r) for x in (has_lo, has_hi)]

    class Exchange:
        def __init__(self, n, buf, w):
            count = [0]

            def item(src, dst, peer, to, frm):
                k = count[0]
                count[0] += 1
                c = pltpu.make_async_remote_copy(
                    src_ref=buf.at[(slice(None),) + src],
                    dst_ref=buf.at[(slice(None),) + dst],
                    send_sem=hs.at[n, k],
                    recv_sem=hr.at[n, k],
                    device_id=peer,
                    device_id_type=MESH,
                )
                return c, to, frm

            down, up = (gx - 1, gy), (gx + 1, gy)
            left, right = (gx, gy - 1), (gx, gy + 1)
            l_src, r_src = pl.ds(W, W), pl.ds(COLS, W)
            l_dst, r_dst = pl.ds(0, W), pl.ds(W + COLS, W)
            parts = (l_src, r_src, pl.ds(2 * W, COLS - 2 * W))
            lo_rows = ((0, HALF), (HALF, w - HALF))
            hi_rows = ((ROWS - HALF, HALF), (ROWS - w, w - HALF))
            self.x = [[], []]
            self.corner = [[], []]
            for r, k in lo_rows:
                src, dst = pl.ds(W + r, k), pl.ds(W + ROWS + r, k)
                self.x[0].append([item((src, p), (dst, p), down, has_lo, has_hi) for p in parts])
            for r, k in hi_rows:
                src, dst = pl.ds(W + r, k), pl.ds(W + r - ROWS, k)
                self.x[1].append([item((src, p), (dst, p), up, has_hi, has_lo) for p in parts])
            for side, rows, shift in ((0, hi_rows, -ROWS), (1, lo_rows, ROWS)):
                with_l, with_r = with_both[side]
                for r, k in rows:
                    at = pl.ds(W + r + shift, k)
                    self.corner[side].append(
                        [
                            item((at, l_src), (at, r_dst), left, with_l, with_r),
                            item((at, r_src), (at, l_dst), right, with_r, with_l),
                        ]
                    )
            self.y = []
            for r, k in ((0, 4), (4, 4), (8, 16), (24, 4), (28, 4)):
                at = pl.ds(W + r, k)
                self.y.append(
                    [
                        item((at, l_src), (at, r_dst), left, has_l, has_r),
                        item((at, r_src), (at, l_dst), right, has_r, has_l),
                    ]
                )
            self.all = sum(self.x[0] + self.x[1] + self.corner[0] + self.corner[1] + self.y, [])

        def send(self, side, c):
            start(self.x[side][c] + self.y[((0, 1), (4, 3))[side][c]])

        def forward(self, side, c):
            recv(self.x[1 - side][c][:2])
            start(self.corner[side][c])

        def finish(self, side, c):
            recv(self.x[1 - side][c][2:] + self.corner[side][c])

    def grouped(items, which, act):
        groups = {}
        for item in items:
            groups.setdefault(id(item[which]), []).append(item)
        for group in groups.values():
            @pl.when(group[0][which])
            def _(group=group):
                for item in group:
                    act(item[0])

    def start(items):
        grouped(items, 1, lambda c: c.start())

    def recv(items):
        grouped(items, 2, lambda c: c.wait_recv())

    def sent(items):
        grouped(items, 1, lambda c: c.wait_send())

    def conv_y(buf, band_ref, yf, order, lo, hi):
        def pair(p, carry):
            x = 2 * p
            for ch, fields in order:
                columns = []
                for j in range(2):
                    h, l = split(buf[ch, x + j])
                    columns.append(jnp.concatenate([h, l, h, h[:16]], 0))
                rhs = jnp.concatenate(columns, 1)
                out = jnp.dot(band_ref[ch], rhs, preferred_element_type=F32)
                for q, f in enumerate(fields):
                    for j in range(2):
                        yf[f, x + j] = out[q * COLS : (q + 1) * COLS, j * DEPTH : (j + 1) * DEPTH]
            return carry

        lax.fori_loop(lo, hi, pair, 0, unroll=2)

    def decaying(rows, n):
        q, q9 = DECAY, DECAY**9
        ahead, behind = [None] * n, [None] * n
        acc = rows[-8]
        for k in range(-7, 1):
            acc = acc * q + rows[k]
        behind[0] = acc
        for x in range(1, n):
            acc = acc * q + (rows[x] - q9 * rows[x - 9])
            behind[x] = acc
        acc = rows[n + 7]
        for k in range(n + 6, n - 1, -1):
            acc = acc * q + rows[k]
        acc = acc * q
        ahead[n - 1] = acc
        for x in range(n - 2, -1, -1):
            acc = (acc + rows[x + 1]) * q - q9 * rows[x + 9]
            ahead[x] = acc
        return [a + b for a, b in zip(ahead, behind)]

    def conv_x(r0, n, yf, specs):
        def chunk(j, carry):
            cols = pl.ds(pl.multiple_of(j * 16, 16), 16)
            for f, taps, radius, kind, comp in specs:
                rows = {i: yf[f, r0 + W + i, cols, :] for i in range(-radius, n + radius)}
                if taps is None:
                    outs = decaying(rows, n)
                else:
                    outs = []
                    for x in range(n):
                        acc = None
                        for k in range(radius + 1):
                            w = taps[8 + k]
                            if w == 0.0:
                                continue
                            v = rows[x] if k == 0 else rows[x + k] + rows[x - k]
                            acc = w * v if acc is None else acc + w * v
                        outs.append(acc)
                for x in range(n):
                    h, l = split(outs[x])
                    at = pl.ds(pl.multiple_of(x * COLS + j * 16, 16), 16)
                    lh[kind, comp, at, pl.ds(0, DEPTH)] = h
                    lh[kind, comp, at, pl.ds(DEPTH, DEPTH)] = l
            return carry

        lax.fori_loop(0, COLS // 16, chunk, 0, unroll=4 if n == HALF else 1)

    def conv_z(kind, comp, n, table):
        v = jnp.dot(lh[kind, comp, pl.ds(0, n * COLS)], table, preferred_element_type=F32)
        return v if v.shape[1] == DEPTH else v[:, :DEPTH] + v[:, DEPTH:]

    specs_a = []
    for c, r in ((0, 5), (1, 7)):
        specs_a.append((c * 3 + 0, x_taps(0, c, SEGMENTS[c]), r, 0, c))
        specs_a.append((c * 3 + 1, x_taps(1, c), r, 1, c))
        specs_a.append((c * 3 + 2, None, 8, 2, c))
    specs_b = []
    for c, r in ((0, 5), (1, 7)):
        specs_b.append((2 + c, x_taps(0, c, SEGMENTS[c]), r, 0, c))
        specs_b.append((c, x_taps(1, c), r, 1, c))

    def convs_a(it, r0, n):
        conv_x(r0, n, yfa, specs_a)
        at = pl.ds(pl.multiple_of(r0 * COLS, HALF * COLS), n * COLS)
        for c in range(2):
            lanes = pl.ds(c * DEPTH, DEPTH)
            cres[it, 0, at, lanes] = conv_z(0, c, n, zp_ref[c])
            cres[it, 1, at, lanes] = conv_z(1, c, n, zs_ref[c])
            cres[it, 2, at, lanes] = conv_z(2, c, n, za_ref[...])

    def derive(it, r0, n, der):
        def row(i, carry):
            x = r0 + i
            at = pl.ds(pl.multiple_of(x * COLS, COLS), COLS)

            def both(kind):
                out = []
                for c in range(2):
                    lanes = pl.ds(c * DEPTH, DEPTH)
                    v = cres[0, kind, at, lanes]
                    if it == 1:
                        v = (1.0 - DAMPING) * v + scl[c, 0:1] * cres[1, kind, at, lanes]
                    out.append(v)
                return out

            p0, p1 = both(0)
            s0, s1 = both(1)
            a0, a1 = both(2)
            t = 1.0 + (p0 + p1)
            n2 = s0 + s1
            der[0, x + W, pl.ds(W, COLS), :] = jnp.log(t) + (2.0 * CROSS) * n2 * t
            der[1, x + W, pl.ds(W, COLS), :] = n2 / t + CROSS * n2 * n2
            for i in range(2):
                att[i, at] = ATTRACT[i][0] * a0 + ATTRACT[i][1] * a1
            return carry

        lax.fori_loop(0, n, row, 0, unroll=2)

    def stage_a(it, r0, n, der):
        convs_a(it, r0, n)
        derive(it, r0, n, der)

    def stage_b(r0, n, dest, off):
        conv_x(r0, n, yfb, specs_b)
        for i in range(2):
            res[i, pl.ds(0, n * COLS)] = conv_z(0, i, n, zp_ref[i]) + conv_z(1, i, n, zs_ref[i])

        def row(x, carry):
            at = pl.ds(pl.multiple_of(x * COLS, COLS), COLS)
            glob = pl.ds(pl.multiple_of((r0 + x) * COLS, COLS), COLS)
            keep = mask[r0 + x] == 0
            for i in range(2):
                v = jnp.where(keep, jnp.exp(att[i, glob] - res[i, at]), 0.0)
                dest[i, r0 + x + off, pl.ds(off, COLS), :] = v
                part = v[0:8]
                for q in range(1, COLS // 8):
                    part = part + v[8 * q : 8 * q + 8]
                tot[i] = tot[i] + part
            return carry

        lax.fori_loop(0, n, row, 0, unroll=2)

    copies = []

    def sum_start(it, s, mine):
        arbuf[it, s] = mine
        out = []
        for d, peer in enumerate(stages[s]):
            c = pltpu.make_async_remote_copy(
                src_ref=arbuf.at[it, s],
                dst_ref=arrecv.at[it, s, d],
                send_sem=as_.at[it, s, d],
                recv_sem=ar_.at[it, s, d],
                device_id=peer,
                device_id_type=MESH,
            )
            c.start()
            out.append(c)
        copies.extend(out)
        return out

    def sum_finish(it, s, mine, out):
        for d in range(len(out) - 1, -1, -1):
            out[d].wait_recv()
            mine = mine + arrecv[it, s, d]
        return mine

    def local_total():
        sums = [jnp.sum(tot[i], axis=0, keepdims=True) for i in range(2)]
        rowid = lax.broadcasted_iota(jnp.int32, (8, DEPTH), 0)
        return jnp.where(rowid == 0, sums[0], jnp.where(rowid == 1, sums[1], 0.0))

    def scales(mine, dest):
        total = jnp.sum(mine, axis=1, keepdims=True)
        for i in range(2):
            dest[i] = jnp.broadcast_to(DAMPING * load_ref[i] * cells / total[i : i + 1], (8, DEPTH))

    order_a = ((0, (0, 1, 2)), (1, (3, 4, 5)))
    order_b = ((0, (0, 1)), (1, (2, 3)))
    x_rho = Exchange(0, rho, W)
    x_der1 = Exchange(1, der1, W - 1)
    x_prp = Exchange(2, prp, W)
    x_der2 = Exchange(3, der2, W - 1)
    pairs = (((2, 4), (0, 2)), ((20, 22), (22, 24)))
    first = ((0, HALF), (ROWS - HALF, ROWS - 2 * HALF))
    sides = (0, 1)

    def inner(stage, between):
        def step(i, carry):
            stage(8 + 8 * i)
            pl.when(i == 0)(between)
            return carry

        lax.fori_loop(0, 2, step, 0)

    def forward(x, c):
        for side in sides:
            x.forward(side, c)

    for c in (NEAR, FAR):
        for side in sides:
            x_rho.send(side, c)
    start(x_rho.y[2])
    for buf in (der1, prp, der2):
        zeros(buf)
    tot[...] = jnp.zeros_like(tot)
    tables[0].wait()
    recv(sum(x_rho.y, []))
    conv_y(rho, ya_ref, yfa, order_a, 4, 12)
    for side in sides:
        x_rho.forward(side, NEAR)
    conv_y(rho, ya_ref, yfa, order_a, 12, 20)
    for t in tables[1:4]:
        t.wait()
    inner(lambda r0: stage_a(0, r0, 8, der1), lambda: forward(x_rho, FAR))
    start(x_der1.y[2])
    for side in sides:
        x_rho.finish(side, NEAR)
        conv_y(rho, ya_ref, yfa, order_a, *pairs[side][NEAR])
        stage_a(0, first[side][FAR], HALF, der1)
        x_der1.send(side, FAR)
    for side in sides:
        x_rho.finish(side, FAR)
        conv_y(rho, ya_ref, yfa, order_a, *pairs[side][FAR])
        stage_a(0, first[side][NEAR], HALF, der1)
        x_der1.send(side, NEAR)

    def proposals(x_der, der, dest, off, between, after):
        recv(x_der.y[2])
        conv_y(der, yb_ref, yfb, order_b, 8, 16)
        for side in sides:
            x_der.forward(side, FAR)
        recv(x_der.y[1])
        conv_y(der, yb_ref, yfb, order_b, 6, 8)
        recv(x_der.y[3])
        conv_y(der, yb_ref, yfb, order_b, 16, 18)
        recv(x_der.y[0])
        conv_y(der, yb_ref, yfb, order_b, 4, 6)
        recv(x_der.y[4])
        conv_y(der, yb_ref, yfb, order_b, 18, 20)
        inner(lambda r0: stage_b(r0, 8, dest, off), lambda: forward(x_der, NEAR))
        between()
        for side in sides:
            x_der.finish(side, FAR)
            conv_y(der, yb_ref, yfb, order_b, *pairs[side][FAR])
        for side in sides:
            x_der.finish(side, NEAR)
            conv_y(der, yb_ref, yfb, order_b, *pairs[side][NEAR])
            stage_b(first[side][NEAR], HALF, dest, off)
            after(side, NEAR)
        for side in sides:
            stage_b(first[side][FAR], HALF, dest, off)
            after(side, FAR)

    for t in tables[4:]:
        t.wait()
    proposals(x_der1, der1, prp, W, lambda: start(x_prp.y[2]), x_prp.send)

    mine = local_total()
    tot[...] = jnp.zeros_like(tot)
    out = sum_start(0, 0, mine)
    recv(x_prp.y[2])
    conv_y(prp, ya_ref, yfa, order_a, 8, 16)
    recv(x_prp.y[0] + x_prp.y[4] + x_prp.y[1] + x_prp.y[3])
    conv_y(prp, ya_ref, yfa, order_a, 4, 8)
    for side in sides:
        x_prp.forward(side, NEAR)
    conv_y(prp, ya_ref, yfa, order_a, 16, 20)
    mine = sum_finish(0, 0, mine, out)
    out = sum_start(0, 1, mine)
    inner(lambda r0: convs_a(1, r0, 8), lambda: forward(x_prp, FAR))
    for side in sides:
        x_prp.finish(side, NEAR)
        conv_y(prp, ya_ref, yfa, order_a, *pairs[side][NEAR])
        convs_a(1, first[side][FAR], HALF)
    mine = sum_finish(0, 1, mine, out)
    scales(mine, scl)
    for side in sides:
        derive(1, first[side][FAR], HALF, der2)
        x_der2.send(side, FAR)
    derive(1, 8, 16, der2)
    start(x_der2.y[2])
    for side in sides:
        x_prp.finish(side, FAR)
        conv_y(prp, ya_ref, yfa, order_a, *pairs[side][FAR])
        convs_a(1, first[side][NEAR], HALF)
        derive(1, first[side][NEAR], HALF, der2)
        x_der2.send(side, NEAR)

    def base():
        def row(x, carry):
            for c in range(2):
                new = (1.0 - DAMPING) * rho[c, x + W, pl.ds(W, COLS), :] + scl[c, 0:1] * prp[
                    c, x + W, pl.ds(W, COLS), :
                ]
                base_ref[c, x] = (1.0 - DAMPING) * new
            return carry

        lax.fori_loop(0, ROWS, row, 0)

    proposals(x_der2, der2, prop_ref, 0, base, lambda side, c: None)
    mine = local_total()
    out = sum_start(1, 0, mine)
    sent(x_rho.all + x_der1.all + x_prp.all + x_der2.all)
    mine = sum_finish(1, 0, mine, out)
    out = sum_start(1, 1, mine)
    for c in copies[: -len(out)]:
        c.wait_send()
    mine = sum_finish(1, 1, mine, out)
    scales(mine, scl_ref)
    for c in out:
        c.wait_send()


def last_kernel(base_ref, prop_ref, scl_ref, out_hbm, buf, sem):
    step = 8
    copies = []
    for x in range(0, ROWS, step):

        def row(i, carry):
            for c in range(2):
                buf[c, i] = base_ref[c, i] + scl_ref[c, 0:1] * prop_ref[c, i]
            return carry

        lax.fori_loop(x, x + step, row, 0)
        at = pl.ds(x, step)
        c = pltpu.make_async_copy(buf.at[:, at], out_hbm.at[:, at], sem.at[x // step])
        c.start()
        copies.append(c)
    for c in copies:
        c.wait()


def body(density_init, solid_mask, loadings):
    consts = [jnp.asarray(c) for c in constants()]
    anyspace = pl.BlockSpec(memory_space=pl.ANY)
    vmem = pl.BlockSpec(memory_space=pltpu.VMEM)
    smem = pl.BlockSpec(memory_space=pltpu.SMEM)
    padded = pltpu.VMEM((2, PR, PC, DEPTH), F32)
    field = pltpu.VMEM((2, ROWS, COLS, DEPTH), F32)
    dma = pltpu.SemaphoreType.DMA
    base, prop, scl = pl.pallas_call(
        kernel,
        out_shape=(field, field, pltpu.VMEM((2, 8, DEPTH), F32)),
        in_specs=[anyspace, anyspace, smem] + [anyspace] * len(consts),
        out_specs=(vmem, vmem, vmem),
        scratch_shapes=[
            padded, padded, padded, padded,
            pltpu.VMEM((ROWS, COLS, DEPTH), jnp.int32),
            pltpu.VMEM((6, PR, COLS, DEPTH), F32),
            pltpu.VMEM((4, PR, COLS, DEPTH), F32),
            pltpu.VMEM((3, 2, BLK * COLS, 2 * DEPTH), BF16),
            pltpu.VMEM((2, BLK * COLS, DEPTH), F32),
            pltpu.VMEM((2, 3, ROWS * COLS, 2 * DEPTH), F32),
            pltpu.VMEM((2, ROWS * COLS, DEPTH), F32),
            pltpu.VMEM((2, 8, DEPTH), F32),
            pltpu.VMEM((2, 8, DEPTH), F32),
            pltpu.VMEM((2, 2, 8, DEPTH), F32),
            pltpu.VMEM((2, 2, 15, 8, DEPTH), F32),
        ]
        + [pltpu.VMEM(c.shape, BF16) for c in consts]
        + [dma((8,)), dma((4, 32)), dma((4, 32)), dma((2, 2, 15)), dma((2, 2, 15))],
        compiler_params=pltpu.CompilerParams(
            collective_id=0, has_side_effects=True, vmem_limit_bytes=54 * 2**20
        ),
        name="picard",
    )(density_init, solid_mask, loadings, *consts)
    return pl.pallas_call(
        last_kernel,
        out_shape=jax.ShapeDtypeStruct((2, ROWS, COLS, DEPTH), F32),
        in_specs=[vmem, vmem, vmem],
        out_specs=anyspace,
        scratch_shapes=[field, dma((4,))],
        compiler_params=pltpu.CompilerParams(vmem_limit_bytes=4 * 2**20),
        name="last",
    )(base, prop, scl)


def solution(mesh):
    in_specs = (P(None, "gx", "gy", None), P("gx", "gy", None), P())
    out_specs = P(None, "gx", "gy", None)
    return jax.shard_map(body, mesh=mesh, in_specs=in_specs, out_specs=out_specs, check_vma=False)
```

```python
import jax
import jax.numpy as jnp
import ml_dtypes
import numpy as np
from jax import lax
from jax.experimental import pallas as pl
from jax.experimental.pallas import tpu as pltpu
from jax.sharding import PartitionSpec as P

SEGMENTS = (1.5131, 1.0)
RADII = (6.0, 8.0)
CROSS = 0.25
DAMPING = 0.3
ATTRACT = ((0.3, 0.22), (0.22, 0.16))

W = 8
ROWS, COLS, DEPTH = 32, 64, 128
PR, PC = ROWS + 2 * W, COLS + 2 * W
BLK = 8
GX, GY, NZ_, NY_ = 32, 8, 8, 4
NEAR, FAR = 0, 1
HALF = 4
DECAY = float(np.exp(-0.25))
MESH = pl.DeviceIdType.MESH
BF16 = jnp.bfloat16
F32 = jnp.float32


def raw_profile(kind, radius):
    k = np.arange(17) - 8.0
    if kind == 0:
        return np.maximum(radius * radius - k * k, 0.0)
    if kind == 1:
        return k * k * np.maximum(radius * radius - k * k, 0.0)
    v = np.exp(-np.abs(k) / 4.0)
    return v / v.sum()


RAW = {(k, c): raw_profile(k, RADII[c]) for k in range(3) for c in range(2)}


def x_taps(kind, comp, extra=1.0):
    v = RAW[kind, comp]
    return (v / v.sum() ** 3 * extra).tolist()


def split_np(table):
    hi = table.astype(np.float32).astype(ml_dtypes.bfloat16)
    lo = (table - hi.astype(np.float64)).astype(np.float32).astype(ml_dtypes.bfloat16)
    return hi, lo


def band_y(profiles):
    tables = []
    for taps in profiles:
        t = np.zeros((COLS, PC))
        for o in range(COLS):
            t[o, o : o + 17] = taps
        tables.append(t)
    hi, lo = split_np(np.concatenate(tables, 0))
    pad = np.zeros((hi.shape[0], 16), ml_dtypes.bfloat16)
    return np.concatenate([hi, hi, lo, pad], 1)


def band_z(taps):
    t = np.zeros((DEPTH, DEPTH))
    for o in range(DEPTH):
        for k in range(17):
            i = o + k - 8
            if 0 <= i < DEPTH:
                t[i, o] = taps[k]
    return t


def wide_z(table):
    hi, lo = split_np(table)
    return np.concatenate(
        [np.concatenate([hi, lo], 1), np.concatenate([hi, np.zeros_like(lo)], 1)], 0
    )


def constants():
    ya = [band_y([RAW[0, c], RAW[1, c], RAW[2, c]]) for c in range(2)]
    yb = [band_y([RAW[k, 0], RAW[k, 1]]) for k in (1, 0)]
    zp = [np.concatenate([split_np(band_z(RAW[0, c]))[0]] * 2, 0) for c in range(2)]
    zs = [wide_z(band_z(RAW[1, c])) for c in range(2)]
    za = wide_z(band_z(RAW[2, 0]) * RAW[2, 0][8])
    return [np.stack(ya), np.stack(yb), np.stack(zp), np.stack(zs), za]


def split(v):
    hi = v.astype(BF16)
    return hi, (v - hi.astype(F32)).astype(BF16)


def kernel(
    dens_hbm, mask_hbm, load_ref, ya_hbm, yb_hbm, zp_hbm, zs_hbm, za_hbm,
    base_ref, prop_ref, scl_ref,
    rho, prp, der1, der2, mask, yfa, yfb, lh, res, cres, att, tot, scl, arbuf, arrecv,
    ya_ref, yb_ref, zp_ref, zs_ref, za_ref,
    in_sem, hs, hr, as_, ar_,
):
    gx, gy = lax.axis_index("gx"), lax.axis_index("gy")
    yy, zz = gx // NZ_, gx % NZ_
    cells = float(ROWS * GX * COLS * GY * DEPTH)

    loads = [
        pltpu.make_async_copy(
            dens_hbm, rho.at[:, pl.ds(W, ROWS), pl.ds(W, COLS), :], in_sem.at[0]
        ),
        pltpu.make_async_copy(mask_hbm, mask, in_sem.at[1]),
    ]
    wanted = (
        (ya_hbm, ya_ref), (zp_hbm, zp_ref), (zs_hbm, zs_ref), (za_hbm, za_ref), (yb_hbm, yb_ref),
    )
    tables = [
        pltpu.make_async_copy(a, b, in_sem.at[2 + i]) for i, (a, b) in enumerate(wanted)
    ]
    for c in loads:
        c.start()

    xx, core = gy // 2, gy % 2
    plane = [(dy, dx) for dy in range(NY_) for dx in range(4) if (dy, dx) != (0, 0)]
    plane.sort(key=lambda p: -(min(p[0], NY_ - p[0]) + min(p[1], 4 - p[1])))
    line = [(dz, dc) for dz in range(NZ_) for dc in range(2) if (dz, dc) != (0, 0)]
    line.sort(key=lambda p: -(2 * min(p[0], NZ_ - p[0]) + p[1]))
    stages = [
        [(((yy + dy) % NY_) * NZ_ + zz, ((xx + dx) % 4) * 2 + core) for dy, dx in plane],
        [(yy * NZ_ + (zz + dz) % NZ_, xx * 2 + (core + dc) % 2) for dz, dc in line],
    ]
    barrier = pltpu.get_barrier_semaphore()
    greeted = 0
    for peers in stages:
        for peer in peers:
            greeted += 1
            pl.semaphore_signal(barrier, inc=1, device_id=peer, device_id_type=MESH)

    has_lo, has_hi = gx > 0, gx < GX - 1
    has_l, has_r = gy > 0, gy < GY - 1

    near = (
        (has_lo, (gx - 1, gy)),
        (has_hi, (gx + 1, gy)),
        (has_l, (gx, gy - 1)),
        (has_r, (gx, gy + 1)),
    )
    for there, peer in near:
        @pl.when(there)
        def _(peer=peer):
            pl.semaphore_signal(barrier, inc=1, device_id=peer, device_id_type=MESH)

    def zeros(buf):
        @pl.when(gx == 0)
        def _():
            buf[:, pl.ds(0, W)] = jnp.zeros((2, W, PC, DEPTH), F32)

        @pl.when(gx == GX - 1)
        def _():
            buf[:, pl.ds(W + ROWS, W)] = jnp.zeros((2, W, PC, DEPTH), F32)

        @pl.when(gy == 0)
        def _():
            buf[:, :, pl.ds(0, W)] = jnp.zeros((2, PR, W, DEPTH), F32)

        @pl.when(gy == GY - 1)
        def _():
            buf[:, :, pl.ds(W + COLS, W)] = jnp.zeros((2, PR, W, DEPTH), F32)

    for c in tables:
        c.start()
    zeros(rho)
    for c in loads:
        c.wait()

    def mask_row(x, carry):
        keep = mask[x] == 0
        for c in range(2):
            v = rho[c, x + W, pl.ds(W, COLS), :]
            rho[c, x + W, pl.ds(W, COLS), :] = jnp.where(keep, v, 0.0)
        return carry

    lax.fori_loop(0, ROWS, mask_row, 0, unroll=2)

    pl.semaphore_wait(
        barrier, greeted + sum(there.astype(jnp.int32) for there, _ in near)
    )

    with_both = [(x & has_l, x & has_r) for x in (has_lo, has_hi)]

    class Exchange:
        def __init__(self, n, buf, w):
            count = [0]

            def item(src, dst, peer, to, frm):
                k = count[0]
                count[0] += 1
                c = pltpu.make_async_remote_copy(
                    src_ref=buf.at[(slice(None),) + src],
                    dst_ref=buf.at[(slice(None),) + dst],
                    send_sem=hs.at[n, k],
                    recv_sem=hr.at[n, k],
                    device_id=peer,
                    device_id_type=MESH,
                )
                return c, to, frm

            down, up = (gx - 1, gy), (gx + 1, gy)
            left, right = (gx, gy - 1), (gx, gy + 1)
            l_src, r_src = pl.ds(W, W), pl.ds(COLS, W)
            l_dst, r_dst = pl.ds(0, W), pl.ds(W + COLS, W)
            parts = (l_src, r_src, pl.ds(2 * W, COLS - 2 * W))
            lo_rows = ((0, HALF), (HALF, w - HALF))
            hi_rows = ((ROWS - HALF, HALF), (ROWS - w, w - HALF))
            self.x = [[], []]
            self.corner = [[], []]
            for r, k in lo_rows:
                src, dst = pl.ds(W + r, k), pl.ds(W + ROWS + r, k)
                self.x[0].append([item((src, p), (dst, p), down, has_lo, has_hi) for p in parts])
            for r, k in hi_rows:
                src, dst = pl.ds(W + r, k), pl.ds(W + r - ROWS, k)
                self.x[1].append([item((src, p), (dst, p), up, has_hi, has_lo) for p in parts])
            for side, rows, shift in ((0, hi_rows, -ROWS), (1, lo_rows, ROWS)):
                with_l, with_r = with_both[side]
                for r, k in rows:
                    at = pl.ds(W + r + shift, k)
                    self.corner[side].append(
                        [
                            item((at, l_src), (at, r_dst), left, with_l, with_r),
                            item((at, r_src), (at, l_dst), right, with_r, with_l),
                        ]
                    )
            self.y = []
            for r, k in ((0, 4), (4, 4), (8, 16), (24, 4), (28, 4)):
                at = pl.ds(W + r, k)
                self.y.append(
                    [
                        item((at, l_src), (at, r_dst), left, has_l, has_r),
                        item((at, r_src), (at, l_dst), right, has_r, has_l),
                    ]
                )
            self.all = sum(self.x[0] + self.x[1] + self.corner[0] + self.corner[1] + self.y, [])

        def send(self, side, c):
            start(self.x[side][c] + self.y[((0, 1), (4, 3))[side][c]])

        def forward(self, side, c):
            recv(self.x[1 - side][c][:2])
            start(self.corner[side][c])

        def finish(self, side, c):
            recv(self.x[1 - side][c][2:] + self.corner[side][c])

    def grouped(items, which, act):
        groups = {}
        for item in items:
            groups.setdefault(id(item[which]), []).append(item)
        for group in groups.values():
            @pl.when(group[0][which])
            def _(group=group):
                for item in group:
                    act(item[0])

    def start(items):
        grouped(items, 1, lambda c: c.start())

    def recv(items):
        grouped(items, 2, lambda c: c.wait_recv())

    def sent(items):
        grouped(items, 1, lambda c: c.wait_send())

    def conv_y(buf, band_ref, yf, order, lo, hi):
        def pair(p, carry):
            x = 2 * p
            for ch, fields in order:
                columns = []
                for j in range(2):
                    h, l = split(buf[ch, x + j])
                    columns.append(jnp.concatenate([h, l, h, h[:16]], 0))
                rhs = jnp.concatenate(columns, 1)
                out = jnp.dot(band_ref[ch], rhs, preferred_element_type=F32)
                for q, f in enumerate(fields):
                    for j in range(2):
                        yf[f, x + j] = out[q * COLS : (q + 1) * COLS, j * DEPTH : (j + 1) * DEPTH]
            return carry

        lax.fori_loop(lo, hi, pair, 0, unroll=2)

    def decaying(rows, n):
        q, q9 = DECAY, DECAY**9
        ahead, behind = [None] * n, [None] * n
        acc = rows[-8]
        for k in range(-7, 1):
            acc = acc * q + rows[k]
        behind[0] = acc
        for x in range(1, n):
            acc = acc * q + (rows[x] - q9 * rows[x - 9])
            behind[x] = acc
        acc = rows[n + 7]
        for k in range(n + 6, n - 1, -1):
            acc = acc * q + rows[k]
        acc = acc * q
        ahead[n - 1] = acc
        for x in range(n - 2, -1, -1):
            acc = (acc + rows[x + 1]) * q - q9 * rows[x + 9]
            ahead[x] = acc
        return [a + b for a, b in zip(ahead, behind)]

    def conv_x(r0, n, yf, specs):
        def chunk(j, carry):
            cols = pl.ds(pl.multiple_of(j * 16, 16), 16)
            for f, taps, radius, kind, comp in specs:
                rows = {i: yf[f, r0 + W + i, cols, :] for i in range(-radius, n + radius)}
                if taps is None:
                    outs = decaying(rows, n)
                else:
                    outs = []
                    for x in range(n):
                        acc = None
                        for k in range(radius + 1):
                            w = taps[8 + k]
                            if w == 0.0:
                                continue
                            v = rows[x] if k == 0 else rows[x + k] + rows[x - k]
                            acc = w * v if acc is None else acc + w * v
                        outs.append(acc)
                for x in range(n):
                    h, l = split(outs[x])
                    at = pl.ds(pl.multiple_of(x * COLS + j * 16, 16), 16)
                    lh[kind, comp, at, pl.ds(0, DEPTH)] = h
                    lh[kind, comp, at, pl.ds(DEPTH, DEPTH)] = l
            return carry

        lax.fori_loop(0, COLS // 16, chunk, 0, unroll=4 if n == HALF else 2)

    def conv_z(kind, comp, n, table):
        v = jnp.dot(lh[kind, comp, pl.ds(0, n * COLS)], table, preferred_element_type=F32)
        return v if v.shape[1] == DEPTH else v[:, :DEPTH] + v[:, DEPTH:]

    specs_a = []
    for c, r in ((0, 5), (1, 7)):
        specs_a.append((c * 3 + 0, x_taps(0, c, SEGMENTS[c]), r, 0, c))
        specs_a.append((c * 3 + 1, x_taps(1, c), r, 1, c))
        specs_a.append((c * 3 + 2, None, 8, 2, c))
    specs_b = []
    for c, r in ((0, 5), (1, 7)):
        specs_b.append((2 + c, x_taps(0, c, SEGMENTS[c]), r, 0, c))
        specs_b.append((c, x_taps(1, c), r, 1, c))

    def convs_a(it, r0, n):
        conv_x(r0, n, yfa, specs_a)
        at = pl.ds(pl.multiple_of(r0 * COLS, HALF * COLS), n * COLS)
        for c in range(2):
            lanes = pl.ds(c * DEPTH, DEPTH)
            cres[it, 0, at, lanes] = conv_z(0, c, n, zp_ref[c])
            cres[it, 1, at, lanes] = conv_z(1, c, n, zs_ref[c])
            cres[it, 2, at, lanes] = conv_z(2, c, n, za_ref[...])

    def derive(it, r0, n, der):
        def row(i, carry):
            x = r0 + i
            at = pl.ds(pl.multiple_of(x * COLS, COLS), COLS)

            def both(kind):
                out = []
                for c in range(2):
                    lanes = pl.ds(c * DEPTH, DEPTH)
                    v = cres[0, kind, at, lanes]
                    if it == 1:
                        v = (1.0 - DAMPING) * v + scl[c, 0:1] * cres[1, kind, at, lanes]
                    out.append(v)
                return out

            p0, p1 = both(0)
            s0, s1 = both(1)
            a0, a1 = both(2)
            t = 1.0 + (p0 + p1)
            n2 = s0 + s1
            der[0, x + W, pl.ds(W, COLS), :] = jnp.log(t) + (2.0 * CROSS) * n2 * t
            der[1, x + W, pl.ds(W, COLS), :] = n2 / t + CROSS * n2 * n2
            for i in range(2):
                att[i, at] = ATTRACT[i][0] * a0 + ATTRACT[i][1] * a1
            return carry

        lax.fori_loop(0, n, row, 0, unroll=2)

    def stage_a(it, r0, n, der):
        convs_a(it, r0, n)
        derive(it, r0, n, der)

    def stage_b(r0, n, dest, off):
        conv_x(r0, n, yfb, specs_b)
        for i in range(2):
            res[i, pl.ds(0, n * COLS)] = conv_z(0, i, n, zp_ref[i]) + conv_z(1, i, n, zs_ref[i])

        def row(x, carry):
            at = pl.ds(pl.multiple_of(x * COLS, COLS), COLS)
            glob = pl.ds(pl.multiple_of((r0 + x) * COLS, COLS), COLS)
            keep = mask[r0 + x] == 0
            for i in range(2):
                v = jnp.where(keep, jnp.exp(att[i, glob] - res[i, at]), 0.0)
                dest[i, r0 + x + off, pl.ds(off, COLS), :] = v
                part = v[0:8]
                for q in range(1, COLS // 8):
                    part = part + v[8 * q : 8 * q + 8]
                tot[i] = tot[i] + part
            return carry

        lax.fori_loop(0, n, row, 0, unroll=2)

    copies = []

    def sum_start(it, s, mine):
        arbuf[it, s] = mine
        out = []
        for d, peer in enumerate(stages[s]):
            c = pltpu.make_async_remote_copy(
                src_ref=arbuf.at[it, s],
                dst_ref=arrecv.at[it, s, d],
                send_sem=as_.at[it, s, d],
                recv_sem=ar_.at[it, s, d],
                device_id=peer,
                device_id_type=MESH,
            )
            c.start()
            out.append(c)
        copies.extend(out)
        return out

    def sum_finish(it, s, mine, out):
        for d in range(len(out) - 1, -1, -1):
            out[d].wait_recv()
            mine = mine + arrecv[it, s, d]
        return mine

    def local_total():
        sums = [jnp.sum(tot[i], axis=0, keepdims=True) for i in range(2)]
        rowid = lax.broadcasted_iota(jnp.int32, (8, DEPTH), 0)
        return jnp.where(rowid == 0, sums[0], jnp.where(rowid == 1, sums[1], 0.0))

    def scales(mine, dest):
        total = jnp.sum(mine, axis=1, keepdims=True)
        for i in range(2):
            dest[i] = jnp.broadcast_to(DAMPING * load_ref[i] * cells / total[i : i + 1], (8, DEPTH))

    order_a = ((0, (0, 1, 2)), (1, (3, 4, 5)))
    order_b = ((0, (0, 1)), (1, (2, 3)))
    x_rho = Exchange(0, rho, W)
    x_der1 = Exchange(1, der1, W - 1)
    x_prp = Exchange(2, prp, W)
    x_der2 = Exchange(3, der2, W - 1)
    pairs = (((2, 4), (0, 2)), ((20, 22), (22, 24)))
    first = ((0, HALF), (ROWS - HALF, ROWS - 2 * HALF))
    sides = (0, 1)

    def inner(stage, between):
        def step(i, carry):
            stage(8 + 8 * i)
            pl.when(i == 0)(between)
            return carry

        lax.fori_loop(0, 2, step, 0)

    def forward(x, c):
        for side in sides:
            x.forward(side, c)

    for c in (NEAR, FAR):
        for side in sides:
            x_rho.send(side, c)
    start(x_rho.y[2])
    for buf in (der1, prp, der2):
        zeros(buf)
    tot[...] = jnp.zeros_like(tot)
    tables[0].wait()
    recv(sum(x_rho.y, []))
    conv_y(rho, ya_ref, yfa, order_a, 4, 12)
    for side in sides:
        x_rho.forward(side, NEAR)
    conv_y(rho, ya_ref, yfa, order_a, 12, 20)
    for t in tables[1:4]:
        t.wait()
    inner(lambda r0: stage_a(0, r0, 8, der1), lambda: forward(x_rho, FAR))
    start(x_der1.y[2])
    for side in sides:
        x_rho.finish(side, NEAR)
        conv_y(rho, ya_ref, yfa, order_a, *pairs[side][NEAR])
        stage_a(0, first[side][FAR], HALF, der1)
        x_der1.send(side, FAR)
    for side in sides:
        x_rho.finish(side, FAR)
        conv_y(rho, ya_ref, yfa, order_a, *pairs[side][FAR])
        stage_a(0, first[side][NEAR], HALF, der1)
        x_der1.send(side, NEAR)

    def proposals(x_der, der, dest, off, between, after):
        recv(x_der.y[2])
        conv_y(der, yb_ref, yfb, order_b, 8, 16)
        for side in sides:
            x_der.forward(side, FAR)
        recv(x_der.y[1])
        conv_y(der, yb_ref, yfb, order_b, 6, 8)
        recv(x_der.y[3])
        conv_y(der, yb_ref, yfb, order_b, 16, 18)
        recv(x_der.y[0])
        conv_y(der, yb_ref, yfb, order_b, 4, 6)
        recv(x_der.y[4])
        conv_y(der, yb_ref, yfb, order_b, 18, 20)
        inner(lambda r0: stage_b(r0, 8, dest, off), lambda: forward(x_der, NEAR))
        between()
        for side in sides:
            x_der.finish(side, FAR)
            conv_y(der, yb_ref, yfb, order_b, *pairs[side][FAR])
        for side in sides:
            x_der.finish(side, NEAR)
            conv_y(der, yb_ref, yfb, order_b, *pairs[side][NEAR])
            stage_b(first[side][NEAR], HALF, dest, off)
            after(side, NEAR)
        for side in sides:
            stage_b(first[side][FAR], HALF, dest, off)
            after(side, FAR)

    for t in tables[4:]:
        t.wait()
    proposals(x_der1, der1, prp, W, lambda: start(x_prp.y[2]), x_prp.send)

    mine = local_total()
    tot[...] = jnp.zeros_like(tot)
    out = sum_start(0, 0, mine)
    recv(x_prp.y[2])
    conv_y(prp, ya_ref, yfa, order_a, 8, 16)
    recv(x_prp.y[0] + x_prp.y[4] + x_prp.y[1] + x_prp.y[3])
    conv_y(prp, ya_ref, yfa, order_a, 4, 8)
    for side in sides:
        x_prp.forward(side, NEAR)
    conv_y(prp, ya_ref, yfa, order_a, 16, 20)
    mine = sum_finish(0, 0, mine, out)
    out = sum_start(0, 1, mine)
    inner(lambda r0: convs_a(1, r0, 8), lambda: forward(x_prp, FAR))
    for side in sides:
        x_prp.finish(side, NEAR)
        conv_y(prp, ya_ref, yfa, order_a, *pairs[side][NEAR])
        convs_a(1, first[side][FAR], HALF)
        if side == 0:
            mine = sum_finish(0, 1, mine, out)
            scales(mine, scl)
        derive(1, first[side][FAR], HALF, der2)
        x_der2.send(side, FAR)
    derive(1, 8, 16, der2)
    start(x_der2.y[2])
    for side in sides:
        x_prp.finish(side, FAR)
        conv_y(prp, ya_ref, yfa, order_a, *pairs[side][FAR])
        convs_a(1, first[side][NEAR], HALF)
        derive(1, first[side][NEAR], HALF, der2)
        x_der2.send(side, NEAR)

    def base():
        def row(x, carry):
            for c in range(2):
                new = (1.0 - DAMPING) * rho[c, x + W, pl.ds(W, COLS), :] + scl[c, 0:1] * prp[
                    c, x + W, pl.ds(W, COLS), :
                ]
                base_ref[c, x] = (1.0 - DAMPING) * new
            return carry

        lax.fori_loop(0, ROWS, row, 0)

    proposals(x_der2, der2, prop_ref, 0, base, lambda side, c: None)
    mine = local_total()
    out = sum_start(1, 0, mine)
    sent(x_rho.all + x_der1.all + x_prp.all + x_der2.all)
    mine = sum_finish(1, 0, mine, out)
    out = sum_start(1, 1, mine)
    for c in copies[: -len(out)]:
        c.wait_send()
    mine = sum_finish(1, 1, mine, out)
    scales(mine, scl_ref)
    for c in out:
        c.wait_send()


def last_kernel(base_ref, prop_ref, scl_ref, out_hbm, buf, sem):
    step = 8
    copies = []
    for x in range(0, ROWS, step):

        def row(i, carry):
            for c in range(2):
                buf[c, i] = base_ref[c, i] + scl_ref[c, 0:1] * prop_ref[c, i]
            return carry

        lax.fori_loop(x, x + step, row, 0)
        at = pl.ds(x, step)
        c = pltpu.make_async_copy(buf.at[:, at], out_hbm.at[:, at], sem.at[x // step])
        c.start()
        copies.append(c)
    for c in copies:
        c.wait()


def body(density_init, solid_mask, loadings):
    consts = [jnp.asarray(c) for c in constants()]
    anyspace = pl.BlockSpec(memory_space=pl.ANY)
    vmem = pl.BlockSpec(memory_space=pltpu.VMEM)
    smem = pl.BlockSpec(memory_space=pltpu.SMEM)
    padded = pltpu.VMEM((2, PR, PC, DEPTH), F32)
    field = pltpu.VMEM((2, ROWS, COLS, DEPTH), F32)
    dma = pltpu.SemaphoreType.DMA
    base, prop, scl = pl.pallas_call(
        kernel,
        out_shape=(field, field, pltpu.VMEM((2, 8, DEPTH), F32)),
        in_specs=[anyspace, anyspace, smem] + [anyspace] * len(consts),
        out_specs=(vmem, vmem, vmem),
        scratch_shapes=[
            padded, padded, padded, padded,
            pltpu.VMEM((ROWS, COLS, DEPTH), jnp.int32),
            pltpu.VMEM((6, PR, COLS, DEPTH), F32),
            pltpu.VMEM((4, PR, COLS, DEPTH), F32),
            pltpu.VMEM((3, 2, BLK * COLS, 2 * DEPTH), BF16),
            pltpu.VMEM((2, BLK * COLS, DEPTH), F32),
            pltpu.VMEM((2, 3, ROWS * COLS, 2 * DEPTH), F32),
            pltpu.VMEM((2, ROWS * COLS, DEPTH), F32),
            pltpu.VMEM((2, 8, DEPTH), F32),
            pltpu.VMEM((2, 8, DEPTH), F32),
            pltpu.VMEM((2, 2, 8, DEPTH), F32),
            pltpu.VMEM((2, 2, 15, 8, DEPTH), F32),
        ]
        + [pltpu.VMEM(c.shape, BF16) for c in consts]
        + [dma((8,)), dma((4, 32)), dma((4, 32)), dma((2, 2, 15)), dma((2, 2, 15))],
        compiler_params=pltpu.CompilerParams(
            collective_id=0, has_side_effects=True, vmem_limit_bytes=54 * 2**20
        ),
        name="picard",
    )(density_init, solid_mask, loadings, *consts)
    return pl.pallas_call(
        last_kernel,
        out_shape=jax.ShapeDtypeStruct((2, ROWS, COLS, DEPTH), F32),
        in_specs=[vmem, vmem, vmem],
        out_specs=anyspace,
        scratch_shapes=[field, dma((4,))],
        compiler_params=pltpu.CompilerParams(vmem_limit_bytes=4 * 2**20),
        name="last",
    )(base, prop, scl)


def solution(mesh):
    in_specs = (P(None, "gx", "gy", None), P("gx", "gy", None), P())
    out_specs = P(None, "gx", "gy", None)
    return jax.shard_map(body, mesh=mesh, in_specs=in_specs, out_specs=out_specs, check_vma=False)
```
